1024 devices in a mesh: dcn: 4 (over x), blk: 32 (over z, y_hi), head: 8 (over y_lo, core).
Axes of the slice: x: 4, y: 8 (y_hi: 2, y_lo: 4; y = y_hi * 4 + y_lo), z: 16, core: 2. Of those that a mesh axis runs over, the one named last changes fastest.
Arguments:
- queries: bfloat16 [65536, 16, 128], P(('dcn', 'blk'), 'head'), may hold values from -128 to 128
- keys: bfloat16 [65536, 128], P(('dcn', 'blk')), may hold values from -5 to 5
- values: bfloat16 [65536, 128], P(('dcn', 'blk')), may hold values from -6 to 6
- out_grad: bfloat16 [65536, 16, 128], P(('dcn', 'blk'), 'head'), may hold values from -6 to 6
- doc_start: int32 [65536], P(('dcn', 'blk')), may hold values from 0 to 65535, as said below
Outputs:
- q_grad: bfloat16 [65536, 16, 128], P(('dcn', 'blk'), 'head')
- k_grad: bfloat16 [65536, 128], P(('dcn', 'blk', 'head'))
- v_grad: bfloat16 [65536, 128], P(('dcn', 'blk', 'head'))
The draws below stay inside these ranges and needn't reach their ends.
Inputs may be any that keep to these rules, and one draw needn't show every extreme that they name: doc_start is non-decreasing, doc_start[i] <= i, and doc_start[i] is i or doc_start[i - 1]; every document has at most 1024 tokens and some document has exactly 1024.
All inputs are finite; a program needn't handle non-finite values.
Results may differ from the reference program's by a relative error of at most 0.04.
Values may be sent and summed in bfloat16 or wider, within the bound.
A program may use at most 32 MiB of HBM per device.

```python
import jax
import jax.numpy as jnp
from jax import lax

E = 128
H = 16
TOK_DEV = 512
WIN = 2
TOKENS = 65536
DOC_MAX = 1024


def paired_draw(key):
    base = jax.random.fold_in(key, 71)
    kk = jnp.clip(jax.random.normal(jax.random.fold_in(base, 1), (TOKENS, E), jnp.float32), -5.0, 5.0)
    qq = jnp.clip(jax.random.normal(jax.random.fold_in(base, 2), (TOKENS, H, E), jnp.float32), -5.0, 5.0)
    return (qq, kk)


def draw_queries(key, part):
    return paired_draw(key)[0].astype(jnp.bfloat16)


def draw_keys(key, part):
    return paired_draw(key)[1].astype(jnp.bfloat16)


def draw_doc_start(key, part):
    base = jax.random.fold_in(key, 5)
    lengths = jax.random.randint(jax.random.fold_in(base, 1), (TOKENS,), 1, DOC_MAX + 1)
    forced = jax.random.randint(jax.random.fold_in(base, 2), (), 0, 2)
    lengths = jnp.where(jnp.arange(TOKENS) == forced, DOC_MAX, lengths).astype(jnp.int32)
    starts = jnp.cumsum(lengths) - lengths
    positions = jnp.arange(TOKENS, dtype=jnp.int32)
    where_doc = jnp.searchsorted(starts, positions, side='right') - 1
    result = starts[where_doc].astype(jnp.int32)
    return jnp.where(positions == TOKENS - 1, TOKENS - 1, result).astype(jnp.int32)


def block_scale(own_key, shape, shards, least, top_value):
    def one(position, blocks):
        heights = jax.random.uniform(jax.random.fold_in(jax.random.fold_in(own_key, 6), position), (blocks,), jnp.float32, least / len(shards), top_value / len(shards))
        return jnp.repeat(jnp.exp(heights), shape[position] // blocks).reshape((-1,) + (1,) * (len(shape) - position - 1))

    factor_of = one(*shards[0])
    for cut in shards[1:]:
        factor_of = factor_of * one(*cut)
    return factor_of


def gaussian(stream_key, extent, deviation, limit, shards=(), kind=jnp.bfloat16):
    level = block_scale(stream_key, extent, shards, -0.22, 0.18) if shards else 1.0
    entries = jax.random.normal(stream_key, extent, jnp.float32) * deviation * level
    return jnp.minimum(jnp.maximum(entries, -limit), limit).astype(kind)


def setup_inputs(seed: int = 0) -> dict:
    splits = jax.random.split(jax.random.key(seed), 6)
    return {
        "queries": draw_queries(jax.random.fold_in(splits[5], 71), 0),
        "keys": draw_keys(jax.random.fold_in(splits[5], 71), 0),
        "values": gaussian(splits[2], (TOKENS, E), 1.0, 6.0, ((0, 128),)),
        "out_grad": gaussian(splits[3], (TOKENS, H, E), 1.0, 6.0, ((0, 128), (1, 8))),
        "doc_start": draw_doc_start(jax.random.fold_in(splits[5], 71), 0),
    }


def local_grads(q, dout, starts, kwin, value_window, qpos, kpos):
    scale = q.shape[-1] ** -0.5
    visible = (kpos[None, :] >= starts[:, None]) & (kpos[None, :] <= qpos[:, None])
    qf = q.astype(jnp.float32)
    df = dout.astype(jnp.float32)
    kf = kwin.astype(jnp.float32)
    vf = value_window.astype(jnp.float32)
    scores = jnp.einsum('ihe,je->hij', qf, kf) * scale
    top = jnp.max(jnp.where(visible[None], scores, -1e30), axis=-1, keepdims=True)
    expo = jnp.where(visible[None], jnp.exp(scores - top), 0.0)
    lse = top + jnp.log(jnp.sum(expo, axis=-1, keepdims=True))
    prob = jnp.where(visible[None], jnp.exp(scores - lse), 0.0)
    prob_low = prob.astype(jnp.bfloat16)
    plf = prob_low.astype(jnp.float32)
    attended_keys = jnp.einsum('hij,je->ihe', plf, vf)
    delta = jnp.sum(df * attended_keys, axis=-1)
    dprob = jnp.einsum('ihe,je->hij', df, vf)
    dscore = (prob * (dprob - jnp.transpose(delta)[:, :, None])).astype(jnp.bfloat16)
    dsf = dscore.astype(jnp.float32)
    dq = (jnp.einsum('hij,je->ihe', dsf, kf) * scale).astype(jnp.bfloat16)
    dk = jnp.einsum('hij,ihe->je', dsf, qf) * scale
    dv = jnp.einsum('hij,ihe->je', plf, df)
    return dq, jnp.concatenate([dk, dv], axis=1)


def reference(queries, keys, values, out_grad, doc_start):
    window_width = keys.shape[1]
    blocks = TOKENS // TOK_DEV
    window_span = (WIN + 1) * TOK_DEV
    window_margin = WIN * TOK_DEV
    kpad = jnp.concatenate([jnp.zeros((window_margin, window_width), keys.dtype), keys], axis=0)
    value_padded = jnp.concatenate([jnp.zeros((window_margin, window_width), values.dtype), values], axis=0)

    def single_block_rows(block):
        first_position = (block * TOK_DEV).astype(jnp.int32)
        q = lax.dynamic_slice_in_dim(queries, first_position, TOK_DEV, 0)
        dout = lax.dynamic_slice_in_dim(out_grad, first_position, TOK_DEV, 0)
        starts = lax.dynamic_slice_in_dim(doc_start, first_position, TOK_DEV, 0)
        kwin = lax.dynamic_slice_in_dim(kpad, first_position, window_span, 0)
        value_window = lax.dynamic_slice_in_dim(value_padded, first_position, window_span, 0)
        qpos = first_position + jnp.arange(TOK_DEV, dtype=jnp.int32)
        kpos = first_position - window_margin + jnp.arange(window_span, dtype=jnp.int32)
        return local_grads(q, dout, starts, kwin, value_window, qpos, kpos)

    dq, parts = lax.map(single_block_rows, jnp.arange(blocks, dtype=jnp.int32))
    q_grad = dq.reshape(TOKENS, queries.shape[1], window_width)
    parts = parts.reshape(blocks, WIN + 1, TOK_DEV, 2 * window_width)
    total = parts[:, WIN]
    for step in range(1, WIN + 1):
        moved = parts[step:, WIN - step]
        filler = jnp.zeros((step, TOK_DEV, 2 * window_width), jnp.float32)
        total = total + jnp.concatenate([moved, filler], axis=0)
    total = total.reshape(TOKENS, 2 * window_width)
    k_grad = total[:, :window_width].astype(jnp.bfloat16)
    v_grad = total[:, window_width:].astype(jnp.bfloat16)
    return q_grad, k_grad, v_grad
```

```python
import jax
import jax.numpy as jnp
from jax import lax
from jax.sharding import PartitionSpec as P

WIN = 2


def from_behind(block, axis, distance):
    devices = range(lax.axis_size(axis))
    route = [(i - distance, i) for i in devices if i - distance in devices]
    return lax.ppermute(block, axis, route)


def local_grads(q, dout, starts, kwin, value_window, qpos, kpos):
    scale = q.shape[-1] ** (-0.5)
    visible = (kpos[None, :] >= starts[:, None]) & (kpos[None, :] <= qpos[:, None])
    scores = jnp.einsum("ihe,je->hij", q, kwin, preferred_element_type=jnp.float32) * scale
    top = jnp.max(jnp.where(visible[None], scores, -1e30), axis=-1, keepdims=True)
    expo = jnp.where(visible[None], jnp.exp(scores - top), 0.0)
    lse = top + jnp.log(jnp.sum(expo, axis=-1, keepdims=True))
    prob = jnp.where(visible[None], jnp.exp(scores - lse), 0.0)
    prob_low = prob.astype(jnp.bfloat16)
    attended_keys = jnp.einsum(
        "hij,je->ihe", prob_low, value_window, preferred_element_type=jnp.float32
    )
    delta = jnp.sum(dout.astype(jnp.float32) * attended_keys, axis=-1)
    dprob = jnp.einsum("ihe,je->hij", dout, value_window, preferred_element_type=jnp.float32)
    dscore = (prob * (dprob - jnp.transpose(delta)[:, :, None])).astype(jnp.bfloat16)
    dq = (
        jnp.einsum("hij,je->ihe", dscore, kwin, preferred_element_type=jnp.float32) * scale
    ).astype(jnp.bfloat16)
    dk = jnp.einsum("hij,ihe->je", dscore, q, preferred_element_type=jnp.float32) * scale
    dv = jnp.einsum("hij,ihe->je", prob_low, dout, preferred_element_type=jnp.float32)
    return (dq, jnp.concatenate([dk, dv], axis=1))


def body(queries, keys, values, out_grad, doc_start):
    rows = keys.shape[0]
    window_width = keys.shape[1]
    local_heads = queries.shape[1]
    position = lax.axis_index(("dcn", "blk"))
    packed = jnp.stack([keys, values])
    pieces = []
    for step in range(WIN, 0, -1):
        pieces.append(from_behind(packed, ("dcn", "blk"), step))
    pieces.append(packed)
    window = jnp.concatenate(pieces, axis=1)
    window_span = (WIN + 1) * rows
    first_position = position * rows
    qpos = first_position + jnp.arange(rows, dtype=jnp.int32)
    kpos = first_position - WIN * rows + jnp.arange(window_span, dtype=jnp.int32)
    grad_list = []
    terms = jnp.zeros((window_span, 2 * window_width), jnp.float32)
    for single in range(local_heads):
        head_dq, head_terms = local_grads(
            queries[:, single : single + 1],
            out_grad[:, single : single + 1],
            doc_start,
            window[0],
            window[1],
            qpos,
            kpos,
        )
        grad_list.append(head_dq)
        terms = terms + head_terms
    q_grad = jnp.concatenate(grad_list, axis=1)
    parts = lax.axis_size("head")
    piece = rows // parts
    head = lax.axis_index("head")
    chunks = terms.reshape(WIN + 1, parts, piece, 2 * window_width)
    stride = 1
    while stride < parts:
        bit = (head // stride) % 2
        chunks = chunks.reshape(WIN + 1, -1, 2, piece, 2 * window_width)
        keep = lax.dynamic_index_in_dim(chunks, bit, axis=2, keepdims=False)
        send = lax.dynamic_index_in_dim(chunks, 1 - bit, axis=2, keepdims=False)
        route = [(i, i ^ stride) for i in range(parts)]
        chunks = keep + lax.ppermute(send, "head", route)
        stride *= 2
    reduced = chunks.reshape(WIN + 1, piece, 2 * window_width)
    total = reduced[WIN]
    for step in range(1, WIN + 1):
        total = total + from_behind(reduced[WIN - step], ("dcn", "blk"), -step)
    k_grad = total[:, :window_width].astype(jnp.bfloat16)
    v_grad = total[:, window_width:].astype(jnp.bfloat16)
    return (q_grad, k_grad, v_grad)


def solution(mesh):
    in_specs = (
        P(("dcn", "blk"), "head", None),
        P(("dcn", "blk"), None),
        P(("dcn", "blk"), None),
        P(("dcn", "blk"), "head", None),
        P(("dcn", "blk")),
    )
    out_specs = (
        P(("dcn", "blk"), "head", None),
        P(("dcn", "blk", "head"), None),
        P(("dcn", "blk", "head"), None),
    )
    return jax.shard_map(body, mesh=mesh, in_specs=in_specs, out_specs=out_specs, check_vma=False)
```

```python
import jax
import jax.numpy as jnp
from jax import lax
from jax.sharding import PartitionSpec as P

WIN = 2


def from_behind(block, axis, distance):
    devices = range(lax.axis_size(axis))
    route = [(i - distance, i) for i in devices if i - distance in devices]
    return lax.ppermute(block, axis, route)


def mirror(head, parts):
    lanes = parts // 2
    return (lanes - 1 - head // 2) * 2 + head % 2


def nearest_next(block, back=False):
    parts = lax.axis_size("head")
    blocks = lax.axis_size(("dcn", "blk"))
    route = []
    for b in range(blocks - 1):
        for h in range(parts):
            pair = (b * parts + h, (b + 1) * parts + mirror(h, parts))
            route.append(pair[::-1] if back else pair)
    return lax.ppermute(block, ("dcn", "blk", "head"), route)


def local_grads(q, dout, starts, kwin, value_window, qpos, kpos):
    scale = q.shape[-1] ** (-0.5)
    visible = (kpos[None, :] >= starts[:, None]) & (kpos[None, :] <= qpos[:, None])
    scores = jnp.einsum("ihe,je->hij", q, kwin, preferred_element_type=jnp.float32) * scale
    top = jnp.max(jnp.where(visible[None], scores, -1e30), axis=-1, keepdims=True)
    expo = jnp.where(visible[None], jnp.exp(scores - top), 0.0)
    lse = top + jnp.log(jnp.sum(expo, axis=-1, keepdims=True))
    prob = jnp.where(visible[None], jnp.exp(scores - lse), 0.0)
    prob_low = prob.astype(jnp.bfloat16)
    attended_keys = jnp.einsum(
        "hij,je->ihe", prob_low, value_window, preferred_element_type=jnp.float32
    )
    delta = jnp.sum(dout.astype(jnp.float32) * attended_keys, axis=-1)
    dprob = jnp.einsum("ihe,je->hij", dout, value_window, preferred_element_type=jnp.float32)
    dscore = (prob * (dprob - jnp.transpose(delta)[:, :, None])).astype(jnp.bfloat16)
    dq = (
        jnp.einsum("hij,je->ihe", dscore, kwin, preferred_element_type=jnp.float32) * scale
    ).astype(jnp.bfloat16)
    dk = jnp.einsum("hij,ihe->je", dscore, q, preferred_element_type=jnp.float32) * scale
    dv = jnp.einsum("hij,ihe->je", prob_low, dout, preferred_element_type=jnp.float32)
    return (dq, jnp.concatenate([dk, dv], axis=1))


def body(queries, keys, values, out_grad, doc_start):
    rows = keys.shape[0]
    window_width = keys.shape[1]
    local_heads = queries.shape[1]
    position = lax.axis_index(("dcn", "blk"))
    packed = jnp.stack([keys, values])
    pieces = []
    for step in range(WIN, 0, -1):
        if step == 1:
            pieces.append(nearest_next(packed))
        else:
            pieces.append(from_behind(packed, ("dcn", "blk"), step))
    pieces.append(packed)
    window = jnp.concatenate(pieces, axis=1)
    window_span = (WIN + 1) * rows
    first_position = position * rows
    qpos = first_position + jnp.arange(rows, dtype=jnp.int32)
    kpos = first_position - WIN * rows + jnp.arange(window_span, dtype=jnp.int32)
    grad_list = []
    terms = jnp.zeros((window_span, 2 * window_width), jnp.float32)
    for single in range(local_heads):
        head_dq, head_terms = local_grads(
            queries[:, single : single + 1],
            out_grad[:, single : single + 1],
            doc_start,
            window[0],
            window[1],
            qpos,
            kpos,
        )
        grad_list.append(head_dq)
        terms = terms + head_terms
    q_grad = jnp.concatenate(grad_list, axis=1)
    parts = lax.axis_size("head")
    piece = rows // parts
    head = lax.axis_index("head")
    chunks = terms.reshape(WIN + 1, parts, piece, 2 * window_width)
    order = jnp.array([mirror(c, parts) for c in range(parts)], jnp.int32)
    chunks = chunks.at[WIN - 1].set(chunks[WIN - 1][order])
    stride = 1
    while stride < parts:
        bit = (head // stride) % 2
        chunks = chunks.reshape(WIN + 1, -1, 2, piece, 2 * window_width)
        keep = lax.dynamic_index_in_dim(chunks, bit, axis=2, keepdims=False)
        send = lax.dynamic_index_in_dim(chunks, 1 - bit, axis=2, keepdims=False)
        route = [(i, i ^ stride) for i in range(parts)]
        chunks = keep + lax.ppermute(send, "head", route)
        stride *= 2
    reduced = chunks.reshape(WIN + 1, piece, 2 * window_width)
    total = reduced[WIN]
    for step in range(1, WIN + 1):
        if step == 1:
            total = total + nearest_next(reduced[WIN - step], back=True)
        else:
            total = total + from_behind(reduced[WIN - step], ("dcn", "blk"), -step)
    k_grad = total[:, :window_width].astype(jnp.bfloat16)
    v_grad = total[:, window_width:].astype(jnp.bfloat16)
    return (q_grad, k_grad, v_grad)


def solution(mesh):
    in_specs = (
        P(("dcn", "blk"), "head", None),
        P(("dcn", "blk"), None),
        P(("dcn", "blk"), None),
        P(("dcn", "blk"), "head", None),
        P(("dcn", "blk")),
    )
    out_specs = (
        P(("dcn", "blk"), "head", None),
        P(("dcn", "blk", "head"), None),
        P(("dcn", "blk", "head"), None),
    )
    return jax.shard_map(body, mesh=mesh, in_specs=in_specs, out_specs=out_specs, check_vma=False)
```

```python
import jax
import jax.numpy as jnp
from jax import lax
from jax.sharding import PartitionSpec as P
from jax.experimental import pallas as pl
from jax.experimental.pallas import tpu as pltpu

WIN = 2


def from_behind(block, axis, distance):
    devices = range(lax.axis_size(axis))
    route = [(i - distance, i) for i in devices if i - distance in devices]
    return lax.ppermute(block, axis, route)


def mirror(head, parts):
    lanes = parts // 2
    return (lanes - 1 - head // 2) * 2 + head % 2


def nearest_next(block, back=False):
    parts = lax.axis_size("head")
    blocks = lax.axis_size(("dcn", "blk"))
    route = []
    for b in range(blocks - 1):
        for h in range(parts):
            pair = (b * parts + h, (b + 1) * parts + mirror(h, parts))
            route.append(pair[::-1] if back else pair)
    return lax.ppermute(block, ("dcn", "blk", "head"), route)


def head_reduce_kernel(x_ref, o_ref, r1, r2, r3, a1, a2, send_sems, recv_sems):
    mesh_id = pl.DeviceIdType.MESH
    dcn = lax.axis_index("dcn")
    blk = lax.axis_index("blk")
    head = lax.axis_index("head")
    bits = [head % 2, (head // 2) % 2, (head // 4) % 2]
    partners = [head + 1 - 2 * bits[0], head + 2 - 4 * bits[1], head + 4 - 8 * bits[2]]
    barrier = pltpu.get_barrier_semaphore()
    for partner in partners:
        pl.semaphore_signal(barrier, 1, device_id=(dcn, blk, partner), device_id_type=mesh_id)
    pl.semaphore_wait(barrier, 3)
    windows = x_ref.shape[0]
    sources = [x_ref, a1, a2]
    targets = [r1, r2, r3]
    copies = [[None] * windows for _ in range(3)]

    def keep_bit(stage, w):
        if stage > 0 and w == windows - 2:
            return 1 - bits[stage]
        return bits[stage]

    def send(stage, w):
        keep = keep_bit(stage, w)
        copy = pltpu.make_async_remote_copy(
            src_ref=sources[stage].at[w, 1 - keep],
            dst_ref=targets[stage].at[w],
            send_sem=send_sems.at[stage, w],
            recv_sem=recv_sems.at[stage, w],
            device_id=(dcn, blk, partners[stage]),
            device_id_type=mesh_id,
        )
        copy.start()
        copies[stage][w] = copy

    for w in range(windows):
        send(0, w)
    for stage in range(3):
        for w in range(windows):
            copies[stage][w].wait_recv()
            summed = sources[stage][w, keep_bit(stage, w)] + targets[stage][w]
            if stage < 2:
                sources[stage + 1][w] = summed
                send(stage + 1, w)
            else:
                o_ref[w] = summed
    for stage in range(3):
        for w in range(windows):
            copies[stage][w].wait_send()


def head_reduce(chunks):
    windows, rest = chunks.shape[0], chunks.shape[4:]
    f32 = jnp.float32
    return pl.pallas_call(
        head_reduce_kernel,
        out_shape=jax.ShapeDtypeStruct((windows,) + rest, f32),
        in_specs=[pl.BlockSpec(memory_space=pltpu.VMEM)],
        out_specs=pl.BlockSpec(memory_space=pltpu.VMEM),
        scratch_shapes=[
            pltpu.VMEM((windows, 2, 2) + rest, f32),
            pltpu.VMEM((windows, 2) + rest, f32),
            pltpu.VMEM((windows,) + rest, f32),
            pltpu.VMEM((windows, 2, 2) + rest, f32),
            pltpu.VMEM((windows, 2) + rest, f32),
            pltpu.SemaphoreType.DMA((3, windows)),
            pltpu.SemaphoreType.DMA((3, windows)),
        ],
        compiler_params=pltpu.CompilerParams(collective_id=0, has_side_effects=True),
    )(chunks)


def local_grads(q, dout, starts, kwin, value_window, qpos, kpos):
    scale = q.shape[-1] ** (-0.5)
    visible = (kpos[None, :] >= starts[:, None]) & (kpos[None, :] <= qpos[:, None])
    scores = jnp.einsum("ihe,je->hij", q, kwin, preferred_element_type=jnp.float32) * scale
    top = jnp.max(jnp.where(visible[None], scores, -1e30), axis=-1, keepdims=True)
    expo = jnp.where(visible[None], jnp.exp(scores - top), 0.0)
    lse = top + jnp.log(jnp.sum(expo, axis=-1, keepdims=True))
    prob = jnp.where(visible[None], jnp.exp(scores - lse), 0.0)
    prob_low = prob.astype(jnp.bfloat16)
    attended_keys = jnp.einsum(
        "hij,je->ihe", prob_low, value_window, preferred_element_type=jnp.float32
    )
    delta = jnp.sum(dout.astype(jnp.float32) * attended_keys, axis=-1)
    dprob = jnp.einsum("ihe,je->hij", dout, value_window, preferred_element_type=jnp.float32)
    dscore = (prob * (dprob - jnp.transpose(delta)[:, :, None])).astype(jnp.bfloat16)
    dq = (
        jnp.einsum("hij,je->ihe", dscore, kwin, preferred_element_type=jnp.float32) * scale
    ).astype(jnp.bfloat16)
    dk = jnp.einsum("hij,ihe->je", dscore, q, preferred_element_type=jnp.float32) * scale
    dv = jnp.einsum("hij,ihe->je", prob_low, dout, preferred_element_type=jnp.float32)
    return (dq, jnp.concatenate([dk, dv], axis=1))


def body(queries, keys, values, out_grad, doc_start):
    rows = keys.shape[0]
    window_width = keys.shape[1]
    local_heads = queries.shape[1]
    position = lax.axis_index(("dcn", "blk"))
    packed = jnp.stack([keys, values])
    pieces = []
    for step in range(WIN, 0, -1):
        if step == 1:
            pieces.append(nearest_next(packed))
        else:
            pieces.append(from_behind(packed, ("dcn", "blk"), step))
    pieces.append(packed)
    window = jnp.concatenate(pieces, axis=1)
    window_span = (WIN + 1) * rows
    first_position = position * rows
    qpos = first_position + jnp.arange(rows, dtype=jnp.int32)
    kpos = first_position - WIN * rows + jnp.arange(window_span, dtype=jnp.int32)
    grad_list = []
    terms = jnp.zeros((window_span, 2 * window_width), jnp.float32)
    for single in range(local_heads):
        head_dq, head_terms = local_grads(
            queries[:, single : single + 1],
            out_grad[:, single : single + 1],
            doc_start,
            window[0],
            window[1],
            qpos,
            kpos,
        )
        grad_list.append(head_dq)
        terms = terms + head_terms
    q_grad = jnp.concatenate(grad_list, axis=1)
    parts = lax.axis_size("head")
    piece = rows // parts
    head = lax.axis_index("head")
    chunks = terms.reshape(WIN + 1, 2, 2, 2, piece, 2 * window_width)
    chunks = jnp.transpose(chunks, (0, 3, 2, 1, 4, 5))
    reduced = head_reduce(chunks)
    total = reduced[WIN]
    for step in range(1, WIN + 1):
        if step == 1:
            total = total + nearest_next(reduced[WIN - step], back=True)
        else:
            total = total + from_behind(reduced[WIN - step], ("dcn", "blk"), -step)
    k_grad = total[:, :window_width].astype(jnp.bfloat16)
    v_grad = total[:, window_width:].astype(jnp.bfloat16)
    return (q_grad, k_grad, v_grad)


def solution(mesh):
    in_specs = (
        P(("dcn", "blk"), "head", None),
        P(("dcn", "blk"), None),
        P(("dcn", "blk"), None),
        P(("dcn", "blk"), "head", None),
        P(("dcn", "blk")),
    )
    out_specs = (
        P(("dcn", "blk"), "head", None),
        P(("dcn", "blk", "head"), None),
        P(("dcn", "blk", "head"), None),
    )
    return jax.shard_map(body, mesh=mesh, in_specs=in_specs, out_specs=out_specs, check_vma=False)
```

```python
import jax
import jax.numpy as jnp
from jax import lax
from jax.sharding import PartitionSpec as P
from jax.experimental import pallas as pl
from jax.experimental.pallas import tpu as pltpu

WIN = 2


def from_behind(block, axis, distance):
    devices = range(lax.axis_size(axis))
    route = [(i - distance, i) for i in devices if i - distance in devices]
    return lax.ppermute(block, axis, route)


def mirror(head, parts):
    lanes = parts // 2
    return (lanes - 1 - head // 2) * 2 + head % 2


def nearest_next(block, back=False):
    parts = lax.axis_size("head")
    blocks = lax.axis_size(("dcn", "blk"))
    route = []
    for b in range(blocks - 1):
        for h in range(parts):
            pair = (b * parts + h, (b + 1) * parts + mirror(h, parts))
            route.append(pair[::-1] if back else pair)
    return lax.ppermute(block, ("dcn", "blk", "head"), route)


def grad_reduce_kernel(x_ref, k_out, v_out, r1, r2, r3, a1, a2, a3, total, back, sends, recvs):
    mesh_id = pl.DeviceIdType.MESH
    dcn = lax.axis_index("dcn")
    blk = lax.axis_index("blk")
    head = lax.axis_index("head")
    per_dcn = lax.axis_size("blk")
    blocks = lax.axis_size("dcn") * per_dcn
    parts = lax.axis_size("head")
    block = dcn * per_dcn + blk
    bits = [head % 2, (head // 2) % 2, (head // 4) % 2]
    partners = [head + 1 - 2 * bits[0], head + 2 - 4 * bits[1], head + 4 - 8 * bits[2]]
    flipped = mirror(head, parts)

    def device(b, h):
        return (b // per_dcn, b % per_dcn, h)

    back_heads = [flipped if w == WIN - 1 else head for w in range(WIN)]
    sends_back = [block >= WIN - w for w in range(WIN)]
    gets_back = [block + WIN - w < blocks for w in range(WIN)]
    barrier = pltpu.get_barrier_semaphore()
    for partner in partners:
        pl.semaphore_signal(barrier, 1, device_id=(dcn, blk, partner), device_id_type=mesh_id)
    for w in range(WIN):
        distance = WIN - w

        @pl.when(sends_back[w])
        def _():
            pl.semaphore_signal(barrier, 1, device_id=device(block - distance, back_heads[w]), device_id_type=mesh_id)

        @pl.when(gets_back[w])
        def _():
            pl.semaphore_signal(barrier, 1, device_id=device(block + distance, back_heads[w]), device_id_type=mesh_id)

    peers = len(partners)
    for w in range(WIN):
        peers = peers + sends_back[w].astype(jnp.int32) + gets_back[w].astype(jnp.int32)
    pl.semaphore_wait(barrier, peers)

    windows = x_ref.shape[0]
    sources = [x_ref, a1, a2]
    targets = [r1, r2, r3]
    copies = [[None] * windows for _ in range(3)]

    def keep_bit(stage, w):
        if stage > 0 and w == WIN - 1:
            return 1 - bits[stage]
        return bits[stage]

    def send(stage, w):
        keep = keep_bit(stage, w)
        copy = pltpu.make_async_remote_copy(
            src_ref=sources[stage].at[w, 1 - keep],
            dst_ref=targets[stage].at[w],
            send_sem=sends.at[stage, w],
            recv_sem=recvs.at[stage, w],
            device_id=(dcn, blk, partners[stage]),
            device_id_type=mesh_id,
        )
        copy.start()
        copies[stage][w] = copy

    def back_copy(w, b):
        return pltpu.make_async_remote_copy(
            src_ref=a3.at[w],
            dst_ref=back.at[w],
            send_sem=sends.at[3, w],
            recv_sem=recvs.at[3, w],
            device_id=device(b, back_heads[w]),
            device_id_type=mesh_id,
        )

    for w in range(windows):
        send(0, w)
    for stage in range(3):
        for w in range(windows):
            copies[stage][w].wait_recv()
            summed = sources[stage][w, keep_bit(stage, w)] + targets[stage][w]
            if stage < 2:
                sources[stage + 1][w] = summed
                send(stage + 1, w)
            elif w < WIN:
                a3[w] = summed

                @pl.when(sends_back[w])
                def _():
                    back_copy(w, block - (WIN - w)).start()

            else:
                total[...] = summed
    for w in range(WIN - 1, -1, -1):

        @pl.when(gets_back[w])
        def _():
            back_copy(w, block + WIN - w).wait_recv()
            total[...] = total[...] + back[w]

    width = k_out.shape[1]
    k_out[...] = total[:, :width].astype(k_out.dtype)
    v_out[...] = total[:, width:].astype(v_out.dtype)
    for stage in range(3):
        for w in range(windows):
            copies[stage][w].wait_send()
    for w in range(WIN):

        @pl.when(sends_back[w])
        def _():
            back_copy(w, block - (WIN - w)).wait_send()


def grad_reduce(chunks, width, dtype):
    windows, rest = chunks.shape[0], chunks.shape[4:]
    f32 = jnp.float32
    out = jax.ShapeDtypeStruct((rest[0], width), dtype)
    return pl.pallas_call(
        grad_reduce_kernel,
        out_shape=(out, out),
        in_specs=[pl.BlockSpec(memory_space=pltpu.VMEM)],
        out_specs=(pl.BlockSpec(memory_space=pltpu.VMEM), pl.BlockSpec(memory_space=pltpu.VMEM)),
        scratch_shapes=[
            pltpu.VMEM((windows, 2, 2) + rest, f32),
            pltpu.VMEM((windows, 2) + rest, f32),
            pltpu.VMEM((windows,) + rest, f32),
            pltpu.VMEM((windows, 2, 2) + rest, f32),
            pltpu.VMEM((windows, 2) + rest, f32),
            pltpu.VMEM((WIN,) + rest, f32),
            pltpu.VMEM(rest, f32),
            pltpu.VMEM((WIN,) + rest, f32),
            pltpu.SemaphoreType.DMA((4, windows)),
            pltpu.SemaphoreType.DMA((4, windows)),
        ],
        compiler_params=pltpu.CompilerParams(collective_id=0, has_side_effects=True),
    )(chunks)


def local_grads(q, dout, starts, kwin, value_window, qpos, kpos):
    scale = q.shape[-1] ** (-0.5)
    visible = (kpos[None, :] >= starts[:, None]) & (kpos[None, :] <= qpos[:, None])
    scores = jnp.einsum("ihe,je->hij", q, kwin, preferred_element_type=jnp.float32) * scale
    top = jnp.max(jnp.where(visible[None], scores, -1e30), axis=-1, keepdims=True)
    expo = jnp.where(visible[None], jnp.exp(scores - top), 0.0)
    lse = top + jnp.log(jnp.sum(expo, axis=-1, keepdims=True))
    prob = jnp.where(visible[None], jnp.exp(scores - lse), 0.0)
    prob_low = prob.astype(jnp.bfloat16)
    attended_keys = jnp.einsum(
        "hij,je->ihe", prob_low, value_window, preferred_element_type=jnp.float32
    )
    delta = jnp.sum(dout.astype(jnp.float32) * attended_keys, axis=-1)
    dprob = jnp.einsum("ihe,je->hij", dout, value_window, preferred_element_type=jnp.float32)
    dscore = (prob * (dprob - jnp.transpose(delta)[:, :, None])).astype(jnp.bfloat16)
    dq = (
        jnp.einsum("hij,je->ihe", dscore, kwin, preferred_element_type=jnp.float32) * scale
    ).astype(jnp.bfloat16)
    dk = jnp.einsum("hij,ihe->je", dscore, q, preferred_element_type=jnp.float32) * scale
    dv = jnp.einsum("hij,ihe->je", prob_low, dout, preferred_element_type=jnp.float32)
    return (dq, jnp.concatenate([dk, dv], axis=1))


def body(queries, keys, values, out_grad, doc_start):
    rows = keys.shape[0]
    window_width = keys.shape[1]
    local_heads = queries.shape[1]
    position = lax.axis_index(("dcn", "blk"))
    packed = jnp.stack([keys, values])
    pieces = []
    for step in range(WIN, 0, -1):
        if step == 1:
            pieces.append(nearest_next(packed))
        else:
            pieces.append(from_behind(packed, ("dcn", "blk"), step))
    pieces.append(packed)
    window = jnp.concatenate(pieces, axis=1)
    window_span = (WIN + 1) * rows
    first_position = position * rows
    qpos = first_position + jnp.arange(rows, dtype=jnp.int32)
    kpos = first_position - WIN * rows + jnp.arange(window_span, dtype=jnp.int32)
    grad_list = []
    terms = jnp.zeros((window_span, 2 * window_width), jnp.float32)
    for single in range(local_heads):
        head_dq, head_terms = local_grads(
            queries[:, single : single + 1],
            out_grad[:, single : single + 1],
            doc_start,
            window[0],
            window[1],
            qpos,
            kpos,
        )
        grad_list.append(head_dq)
        terms = terms + head_terms
    q_grad = jnp.concatenate(grad_list, axis=1)
    parts = lax.axis_size("head")
    piece = rows // parts
    head = lax.axis_index("head")
    chunks = terms.reshape(WIN + 1, 2, 2, 2, piece, 2 * window_width)
    chunks = jnp.transpose(chunks, (0, 3, 2, 1, 4, 5))
    k_grad, v_grad = grad_reduce(chunks, window_width, jnp.bfloat16)
    return (q_grad, k_grad, v_grad)


def solution(mesh):
    in_specs = (
        P(("dcn", "blk"), "head", None),
        P(("dcn", "blk"), None),
        P(("dcn", "blk"), None),
        P(("dcn", "blk"), "head", None),
        P(("dcn", "blk")),
    )
    out_specs = (
        P(("dcn", "blk"), "head", None),
        P(("dcn", "blk", "head"), None),
        P(("dcn", "blk", "head"), None),
    )
    return jax.shard_map(body, mesh=mesh, in_specs=in_specs, out_specs=out_specs, check_vma=False)
```

```python
import jax
import jax.numpy as jnp
from jax import lax
from jax.sharding import PartitionSpec as P
from jax.experimental import pallas as pl
from jax.experimental.pallas import tpu as pltpu

WIN = 2


def from_behind(block, axis, distance):
    devices = range(lax.axis_size(axis))
    route = [(i - distance, i) for i in devices if i - distance in devices]
    return lax.ppermute(block, axis, route)


def mirror(head, parts):
    lanes = parts // 2
    return (lanes - 1 - head // 2) * 2 + head % 2


def nearest_next(block, back=False):
    parts = lax.axis_size("head")
    blocks = lax.axis_size(("dcn", "blk"))
    route = []
    for b in range(blocks - 1):
        for h in range(parts):
            pair = (b * parts + h, (b + 1) * parts + mirror(h, parts))
            route.append(pair[::-1] if back else pair)
    return lax.ppermute(block, ("dcn", "blk", "head"), route)


def grad_reduce_kernel(x_ref, k_out, v_out, r1, r2, r3, a1, a2, a3, total, back, sends, recvs):
    mesh_id = pl.DeviceIdType.MESH
    dcn = lax.axis_index("dcn")
    blk = lax.axis_index("blk")
    head = lax.axis_index("head")
    per_dcn = lax.axis_size("blk")
    blocks = lax.axis_size("dcn") * per_dcn
    parts = lax.axis_size("head")
    block = dcn * per_dcn + blk
    bits = [head % 2, (head // 2) % 2, (head // 4) % 2]
    partners = [head + 1 - 2 * bits[0], head + 2 - 4 * bits[1], head + 4 - 8 * bits[2]]
    flipped = mirror(head, parts)

    def device(b, h):
        return (b // per_dcn, b % per_dcn, h)

    back_heads = [flipped if w == WIN - 1 else head for w in range(WIN)]
    sends_back = [block >= WIN - w for w in range(WIN)]
    gets_back = [block + WIN - w < blocks for w in range(WIN)]
    barrier = pltpu.get_barrier_semaphore()
    for partner in partners:
        pl.semaphore_signal(barrier, 1, device_id=(dcn, blk, partner), device_id_type=mesh_id)
    for w in range(WIN):
        distance = WIN - w

        @pl.when(sends_back[w])
        def _():
            pl.semaphore_signal(barrier, 1, device_id=device(block - distance, back_heads[w]), device_id_type=mesh_id)

        @pl.when(gets_back[w])
        def _():
            pl.semaphore_signal(barrier, 1, device_id=device(block + distance, back_heads[w]), device_id_type=mesh_id)

    peers = len(partners)
    for w in range(WIN):
        peers = peers + sends_back[w].astype(jnp.int32) + gets_back[w].astype(jnp.int32)
    pl.semaphore_wait(barrier, peers)

    windows = x_ref.shape[0]
    sources = [x_ref, a1, a2]
    targets = [r1, r2, r3]
    copies = [[None] * windows for _ in range(3)]

    def keep_bit(stage, w):
        if stage > 0 and w == WIN - 1:
            return 1 - bits[stage]
        return bits[stage]

    def send(stage, w):
        keep = keep_bit(stage, w)
        copy = pltpu.make_async_remote_copy(
            src_ref=sources[stage].at[w, 1 - keep],
            dst_ref=targets[stage].at[w],
            send_sem=sends.at[stage, w],
            recv_sem=recvs.at[stage, w],
            device_id=(dcn, blk, partners[stage]),
            device_id_type=mesh_id,
        )
        copy.start()
        copies[stage][w] = copy

    def back_copy(w, b):
        return pltpu.make_async_remote_copy(
            src_ref=a3.at[w],
            dst_ref=back.at[w],
            send_sem=sends.at[3, w],
            recv_sem=recvs.at[3, w],
            device_id=device(b, back_heads[w]),
            device_id_type=mesh_id,
        )

    for w in range(windows):
        send(0, w)
    for stage in range(3):
        for w in range(windows):
            copies[stage][w].wait_recv()
            summed = sources[stage][w, keep_bit(stage, w)] + targets[stage][w]
            if stage < 2:
                sources[stage + 1][w] = summed
                send(stage + 1, w)
            elif w < WIN:
                a3[w] = summed

                @pl.when(sends_back[w])
                def _():
                    back_copy(w, block - (WIN - w)).start()

            else:
                total[...] = summed
    for w in range(WIN - 1, -1, -1):

        @pl.when(gets_back[w])
        def _():
            back_copy(w, block + WIN - w).wait_recv()
            total[...] = total[...] + back[w]

    width = k_out.shape[1]
    k_out[...] = total[:, :width].astype(k_out.dtype)
    v_out[...] = total[:, width:].astype(v_out.dtype)
    for stage in range(3):
        for w in range(windows):
            copies[stage][w].wait_send()
    for w in range(WIN):

        @pl.when(sends_back[w])
        def _():
            back_copy(w, block - (WIN - w)).wait_send()


def grad_reduce(chunks, width, dtype):
    windows, rest = chunks.shape[0], chunks.shape[4:]
    f32 = jnp.float32
    out = jax.ShapeDtypeStruct((rest[0], width), dtype)
    return pl.pallas_call(
        grad_reduce_kernel,
        out_shape=(out, out),
        in_specs=[pl.BlockSpec(memory_space=pltpu.VMEM)],
        out_specs=(pl.BlockSpec(memory_space=pltpu.VMEM), pl.BlockSpec(memory_space=pltpu.VMEM)),
        scratch_shapes=[
            pltpu.VMEM((windows, 2, 2) + rest, f32),
            pltpu.VMEM((windows, 2) + rest, f32),
            pltpu.VMEM((windows,) + rest, f32),
            pltpu.VMEM((windows, 2, 2) + rest, f32),
            pltpu.VMEM((windows, 2) + rest, f32),
            pltpu.VMEM((WIN,) + rest, f32),
            pltpu.VMEM(rest, f32),
            pltpu.VMEM((WIN,) + rest, f32),
            pltpu.SemaphoreType.DMA((4, windows)),
            pltpu.SemaphoreType.DMA((4, windows)),
        ],
        compiler_params=pltpu.CompilerParams(collective_id=0, has_side_effects=True),
    )(chunks)


def local_grads(q, dout, starts, kwin, value_window, qpos, kpos):
    scale = q.shape[-1] ** (-0.5)
    visible = (kpos[None, :] >= starts[:, None]) & (kpos[None, :] <= qpos[:, None])
    scores = jnp.einsum("ihe,je->hij", q, kwin, preferred_element_type=jnp.float32) * scale
    top = jnp.max(jnp.where(visible[None], scores, -1e30), axis=-1, keepdims=True)
    expo = jnp.where(visible[None], jnp.exp(scores - top), 0.0)
    lse = top + jnp.log(jnp.sum(expo, axis=-1, keepdims=True))
    prob = jnp.where(visible[None], jnp.exp(scores - lse), 0.0)
    prob_low = prob.astype(jnp.bfloat16)
    attended_keys = jnp.einsum(
        "hij,je->ihe", prob_low, value_window, preferred_element_type=jnp.float32
    )
    delta = jnp.sum(dout.astype(jnp.float32) * attended_keys, axis=-1)
    dprob = jnp.einsum("ihe,je->hij", dout, value_window, preferred_element_type=jnp.float32)
    dscore = (prob * (dprob - jnp.transpose(delta)[:, :, None])).astype(jnp.bfloat16)
    dq = (
        jnp.einsum("hij,je->ihe", dscore, kwin, preferred_element_type=jnp.float32) * scale
    ).astype(jnp.bfloat16)
    dk = jnp.einsum("hij,ihe->je", dscore, q, preferred_element_type=jnp.float32) * scale
    dv = jnp.einsum("hij,ihe->je", prob_low, dout, preferred_element_type=jnp.float32)
    return (dq, jnp.concatenate([dk, dv], axis=1))


def body(queries, keys, values, out_grad, doc_start):
    rows = keys.shape[0]
    window_width = keys.shape[1]
    local_heads = queries.shape[1]
    position = lax.axis_index(("dcn", "blk"))
    packed = jnp.stack([keys, values])
    pieces = []
    for step in range(WIN, 0, -1):
        if step == 1:
            pieces.append(nearest_next(packed))
        else:
            pieces.append(from_behind(packed, ("dcn", "blk"), step))
    pieces.append(packed)
    window = jnp.concatenate(pieces, axis=1)
    window_span = (WIN + 1) * rows
    first_position = position * rows
    qpos = first_position + jnp.arange(rows, dtype=jnp.int32)
    kpos = first_position - WIN * rows + jnp.arange(window_span, dtype=jnp.int32)
    q_grad, terms = local_grads(queries, out_grad, doc_start, window[0], window[1], qpos, kpos)
    parts = lax.axis_size("head")
    piece = rows // parts
    head = lax.axis_index("head")
    chunks = terms.reshape(WIN + 1, 2, 2, 2, piece, 2 * window_width)
    chunks = jnp.transpose(chunks, (0, 3, 2, 1, 4, 5))
    k_grad, v_grad = grad_reduce(chunks, window_width, jnp.bfloat16)
    return (q_grad, k_grad, v_grad)


def solution(mesh):
    in_specs = (
        P(("dcn", "blk"), "head", None),
        P(("dcn", "blk"), None),
        P(("dcn", "blk"), None),
        P(("dcn", "blk"), "head", None),
        P(("dcn", "blk")),
    )
    out_specs = (
        P(("dcn", "blk"), "head", None),
        P(("dcn", "blk", "head"), None),
        P(("dcn", "blk", "head"), None),
    )
    return jax.shard_map(body, mesh=mesh, in_specs=in_specs, out_specs=out_specs, check_vma=False)
```

```python
import jax
import jax.numpy as jnp
from jax import lax
from jax.sharding import PartitionSpec as P
from jax.experimental import pallas as pl
from jax.experimental.pallas import tpu as pltpu

WIN = 2


def from_behind(block, axis, distance):
    devices = range(lax.axis_size(axis))
    route = [(i - distance, i) for i in devices if i - distance in devices]
    return lax.ppermute(block, axis, route)


def mirror(head, parts):
    lanes = parts // 2
    return (lanes - 1 - head // 2) * 2 + head % 2


def nearest_next(block, back=False):
    parts = lax.axis_size("head")
    blocks = lax.axis_size(("dcn", "blk"))
    route = []
    for b in range(blocks - 1):
        for h in range(parts):
            pair = (b * parts + h, (b + 1) * parts + mirror(h, parts))
            route.append(pair[::-1] if back else pair)
    return lax.ppermute(block, ("dcn", "blk", "head"), route)


def grad_reduce_kernel(x_ref, k_out, v_out, r1, r2, r3, a1, a2, a3, total, back, sends, recvs):
    mesh_id = pl.DeviceIdType.MESH
    dcn = lax.axis_index("dcn")
    blk = lax.axis_index("blk")
    head = lax.axis_index("head")
    per_dcn = lax.axis_size("blk")
    blocks = lax.axis_size("dcn") * per_dcn
    parts = lax.axis_size("head")
    block = dcn * per_dcn + blk
    bits = [head % 2, (head // 2) % 2, (head // 4) % 2]
    partners = [head + 1 - 2 * bits[0], head + 2 - 4 * bits[1], head + 4 - 8 * bits[2]]
    flipped = mirror(head, parts)

    def device(b, h):
        return (b // per_dcn, b % per_dcn, h)

    back_heads = [flipped if w == WIN - 1 else head for w in range(WIN)]
    sends_back = [block >= WIN - w for w in range(WIN)]
    gets_back = [block + WIN - w < blocks for w in range(WIN)]
    barrier = pltpu.get_barrier_semaphore()
    for partner in partners:
        pl.semaphore_signal(barrier, 1, device_id=(dcn, blk, partner), device_id_type=mesh_id)
    for w in range(WIN):
        distance = WIN - w

        @pl.when(sends_back[w])
        def _():
            pl.semaphore_signal(barrier, 1, device_id=device(block - distance, back_heads[w]), device_id_type=mesh_id)

        @pl.when(gets_back[w])
        def _():
            pl.semaphore_signal(barrier, 1, device_id=device(block + distance, back_heads[w]), device_id_type=mesh_id)

    peers = len(partners)
    for w in range(WIN):
        peers = peers + sends_back[w].astype(jnp.int32) + gets_back[w].astype(jnp.int32)
    pl.semaphore_wait(barrier, peers)

    windows = x_ref.shape[0]
    sources = [x_ref, a1, a2]
    targets = [r1, r2, r3]
    copies = [[None] * windows for _ in range(3)]

    def keep_bit(stage, w):
        if stage > 0 and w == WIN - 1:
            return 1 - bits[stage]
        return bits[stage]

    def send(stage, w):
        keep = keep_bit(stage, w)
        copy = pltpu.make_async_remote_copy(
            src_ref=sources[stage].at[w, 1 - keep],
            dst_ref=targets[stage].at[w],
            send_sem=sends.at[stage, w],
            recv_sem=recvs.at[stage, w],
            device_id=(dcn, blk, partners[stage]),
            device_id_type=mesh_id,
        )
        copy.start()
        copies[stage][w] = copy

    def back_copy(w, b):
        return pltpu.make_async_remote_copy(
            src_ref=a3.at[w],
            dst_ref=back.at[w],
            send_sem=sends.at[3, w],
            recv_sem=recvs.at[3, w],
            device_id=device(b, back_heads[w]),
            device_id_type=mesh_id,
        )

    for w in range(windows):
        send(0, w)
    for stage in range(3):
        for w in range(windows):
            copies[stage][w].wait_recv()
            summed = sources[stage][w, keep_bit(stage, w)] + targets[stage][w]
            if stage < 2:
                sources[stage + 1][w] = summed
                send(stage + 1, w)
            elif w < WIN:
                a3[w] = summed

                @pl.when(sends_back[w])
                def _():
                    back_copy(w, block - (WIN - w)).start()

            else:
                total[...] = summed
    for w in range(WIN - 1, -1, -1):

        @pl.when(gets_back[w])
        def _():
            back_copy(w, block + WIN - w).wait_recv()
            total[...] = total[...] + back[w]

    width = k_out.shape[1]
    k_out[...] = total[:, :width].astype(k_out.dtype)
    v_out[...] = total[:, width:].astype(v_out.dtype)
    for stage in range(3):
        for w in range(windows):
            copies[stage][w].wait_send()
    for w in range(WIN):

        @pl.when(sends_back[w])
        def _():
            back_copy(w, block - (WIN - w)).wait_send()


def grad_reduce(chunks, width, dtype):
    windows, rest = chunks.shape[0], chunks.shape[4:]
    f32 = jnp.float32
    out = jax.ShapeDtypeStruct((rest[0], width), dtype)
    return pl.pallas_call(
        grad_reduce_kernel,
        out_shape=(out, out),
        in_specs=[pl.BlockSpec(memory_space=pltpu.VMEM)],
        out_specs=(pl.BlockSpec(memory_space=pltpu.VMEM), pl.BlockSpec(memory_space=pltpu.VMEM)),
        scratch_shapes=[
            pltpu.VMEM((windows, 2, 2) + rest, f32),
            pltpu.VMEM((windows, 2) + rest, f32),
            pltpu.VMEM((windows,) + rest, f32),
            pltpu.VMEM((windows, 2, 2) + rest, f32),
            pltpu.VMEM((windows, 2) + rest, f32),
            pltpu.VMEM((WIN,) + rest, f32),
            pltpu.VMEM(rest, f32),
            pltpu.VMEM((WIN,) + rest, f32),
            pltpu.SemaphoreType.DMA((4, windows)),
            pltpu.SemaphoreType.DMA((4, windows)),
        ],
        compiler_params=pltpu.CompilerParams(collective_id=0, has_side_effects=True),
    )(chunks)


def attention_kernel(q_ref, d_ref, k_ref, v_ref, s_ref, dq_ref, t_ref, dk_acc, dv_acc):
    heads, rows, width = q_ref.shape
    span = k_ref.shape[0]
    tile = 128
    reach = min(span, WIN * rows + tile)
    scale = width ** (-0.5)
    f32 = jnp.float32
    dk_acc[...] = jnp.zeros_like(dk_acc)
    dv_acc[...] = jnp.zeros_like(dv_acc)
    contract_last = (((1,), (1,)), ((), ()))
    contract_first = (((0,), (0,)), ((), ()))
    for h in range(heads):
        for r0 in range(0, rows, tile):
            k0 = min(r0, span - reach)
            qt = q_ref[h, r0 : r0 + tile, :]
            dt = d_ref[h, r0 : r0 + tile, :]
            kt = k_ref[k0 : k0 + reach, :]
            vt = v_ref[k0 : k0 + reach, :]
            starts = s_ref[r0 : r0 + tile, :]
            row = r0 + lax.broadcasted_iota(jnp.int32, (tile, reach), 0)
            col = k0 + lax.broadcasted_iota(jnp.int32, (tile, reach), 1)
            visible = (col >= starts) & (col <= row + WIN * rows)
            scores = lax.dot_general(qt, kt, contract_last, preferred_element_type=f32) * scale
            top = jnp.max(jnp.where(visible, scores, -1e30), axis=1, keepdims=True)
            expo = jnp.where(visible, jnp.exp(scores - top), 0.0)
            lse = top + jnp.log(jnp.sum(expo, axis=1, keepdims=True))
            prob = jnp.where(visible, jnp.exp(scores - lse), 0.0)
            prob_low = prob.astype(jnp.bfloat16)
            attended = jnp.dot(prob_low, vt, preferred_element_type=f32)
            delta = jnp.sum(dt.astype(f32) * attended, axis=1, keepdims=True)
            dprob = lax.dot_general(dt, vt, contract_last, preferred_element_type=f32)
            dscore = (prob * (dprob - delta)).astype(jnp.bfloat16)
            dq = jnp.dot(dscore, kt, preferred_element_type=f32) * scale
            dq_ref[h, r0 : r0 + tile, :] = dq.astype(dq_ref.dtype)
            dk_acc[k0 : k0 + reach, :] += lax.dot_general(dscore, qt, contract_first, preferred_element_type=f32)
            dv_acc[k0 : k0 + reach, :] += lax.dot_general(prob_low, dt, contract_first, preferred_element_type=f32)
    piece = t_ref.shape[4]
    for w in range(t_ref.shape[0]):
        for c in range(rows // piece):
            first = w * rows + c * piece
            place = (w, c % 2, (c // 2) % 2, c // 4)
            t_ref[place + (slice(None), slice(0, width))] = dk_acc[first : first + piece, :] * scale
            t_ref[place + (slice(None), slice(width, 2 * width))] = dv_acc[first : first + piece, :]


def attention(q, dout, kwin, vwin, starts, parts):
    heads, rows, width = q.shape
    span = kwin.shape[0]
    f32 = jnp.float32
    piece = rows // parts
    vmem = pl.BlockSpec(memory_space=pltpu.VMEM)
    return pl.pallas_call(
        attention_kernel,
        out_shape=(
            jax.ShapeDtypeStruct(q.shape, q.dtype),
            jax.ShapeDtypeStruct((span // rows, 2, 2, 2, piece, 2 * width), f32),
        ),
        in_specs=[vmem] * 5,
        out_specs=(vmem, vmem),
        scratch_shapes=[pltpu.VMEM((span, width), f32), pltpu.VMEM((span, width), f32)],
    )(q, dout, kwin, vwin, starts)


def local_grads(q, dout, starts, kwin, value_window, qpos, kpos):
    scale = q.shape[-1] ** (-0.5)
    visible = (kpos[None, :] >= starts[:, None]) & (kpos[None, :] <= qpos[:, None])
    scores = jnp.einsum("ihe,je->hij", q, kwin, preferred_element_type=jnp.float32) * scale
    top = jnp.max(jnp.where(visible[None], scores, -1e30), axis=-1, keepdims=True)
    expo = jnp.where(visible[None], jnp.exp(scores - top), 0.0)
    lse = top + jnp.log(jnp.sum(expo, axis=-1, keepdims=True))
    prob = jnp.where(visible[None], jnp.exp(scores - lse), 0.0)
    prob_low = prob.astype(jnp.bfloat16)
    attended_keys = jnp.einsum(
        "hij,je->ihe", prob_low, value_window, preferred_element_type=jnp.float32
    )
    delta = jnp.sum(dout.astype(jnp.float32) * attended_keys, axis=-1)
    dprob = jnp.einsum("ihe,je->hij", dout, value_window, preferred_element_type=jnp.float32)
    dscore = (prob * (dprob - jnp.transpose(delta)[:, :, None])).astype(jnp.bfloat16)
    dq = (
        jnp.einsum("hij,je->ihe", dscore, kwin, preferred_element_type=jnp.float32) * scale
    ).astype(jnp.bfloat16)
    dk = jnp.einsum("hij,ihe->je", dscore, q, preferred_element_type=jnp.float32) * scale
    dv = jnp.einsum("hij,ihe->je", prob_low, dout, preferred_element_type=jnp.float32)
    return (dq, jnp.concatenate([dk, dv], axis=1))


def body(queries, keys, values, out_grad, doc_start):
    rows = keys.shape[0]
    window_width = keys.shape[1]
    local_heads = queries.shape[1]
    position = lax.axis_index(("dcn", "blk"))
    packed = jnp.stack([keys, values])
    pieces = []
    for step in range(WIN, 0, -1):
        if step == 1:
            pieces.append(nearest_next(packed))
        else:
            pieces.append(from_behind(packed, ("dcn", "blk"), step))
    pieces.append(packed)
    window = jnp.concatenate(pieces, axis=1)
    window_span = (WIN + 1) * rows
    first_position = position * rows
    qpos = first_position + jnp.arange(rows, dtype=jnp.int32)
    kpos = first_position - WIN * rows + jnp.arange(window_span, dtype=jnp.int32)
    parts = lax.axis_size("head")
    window_start = first_position - WIN * rows
    starts = (doc_start - window_start).reshape(rows, 1)
    dq, chunks = attention(
        jnp.transpose(queries, (1, 0, 2)),
        jnp.transpose(out_grad, (1, 0, 2)),
        window[0],
        window[1],
        starts,
        parts,
    )
    q_grad = jnp.transpose(dq, (1, 0, 2))
    k_grad, v_grad = grad_reduce(chunks, window_width, jnp.bfloat16)
    return (q_grad, k_grad, v_grad)


def solution(mesh):
    in_specs = (
        P(("dcn", "blk"), "head", None),
        P(("dcn", "blk"), None),
        P(("dcn", "blk"), None),
        P(("dcn", "blk"), "head", None),
        P(("dcn", "blk")),
    )
    out_specs = (
        P(("dcn", "blk"), "head", None),
        P(("dcn", "blk", "head"), None),
        P(("dcn", "blk", "head"), None),
    )
    return jax.shard_map(body, mesh=mesh, in_specs=in_specs, out_specs=out_specs, check_vma=False)
```

```python
import jax
import jax.numpy as jnp
from jax import lax
from jax.sharding import PartitionSpec as P
from jax.experimental import pallas as pl
from jax.experimental.pallas import tpu as pltpu

WIN = 2


def from_behind(block, axis, distance):
    devices = range(lax.axis_size(axis))
    route = [(i - distance, i) for i in devices if i - distance in devices]
    return lax.ppermute(block, axis, route)


def mirror(head, parts):
    lanes = parts // 2
    return (lanes - 1 - head // 2) * 2 + head % 2


def nearest_next(block, back=False):
    parts = lax.axis_size("head")
    blocks = lax.axis_size(("dcn", "blk"))
    route = []
    for b in range(blocks - 1):
        for h in range(parts):
            pair = (b * parts + h, (b + 1) * parts + mirror(h, parts))
            route.append(pair[::-1] if back else pair)
    return lax.ppermute(block, ("dcn", "blk", "head"), route)


def grad_reduce_kernel(x_ref, k_out, v_out, r1, r2, r3, a1, a2, t1, t2, a3, total, back, sends, recvs):
    mesh_id = pl.DeviceIdType.MESH
    dcn = lax.axis_index("dcn")
    blk = lax.axis_index("blk")
    head = lax.axis_index("head")
    per_dcn = lax.axis_size("blk")
    blocks = lax.axis_size("dcn") * per_dcn
    parts = lax.axis_size("head")
    block = dcn * per_dcn + blk
    bits = [head % 2, (head // 2) % 2, (head // 4) % 2]
    partners = [head + 1 - 2 * bits[0], head + 2 - 4 * bits[1], head + 4 - 8 * bits[2]]
    flipped = mirror(head, parts)

    def device(b, h):
        return (b // per_dcn, b % per_dcn, h)

    back_heads = [flipped if w == WIN - 1 else head for w in range(WIN)]
    sends_back = [block >= WIN - w for w in range(WIN)]
    gets_back = [block + WIN - w < blocks for w in range(WIN)]
    barrier = pltpu.get_barrier_semaphore()
    for partner in partners:
        pl.semaphore_signal(barrier, 1, device_id=(dcn, blk, partner), device_id_type=mesh_id)
    for w in range(WIN):
        distance = WIN - w

        @pl.when(sends_back[w])
        def _():
            pl.semaphore_signal(barrier, 1, device_id=device(block - distance, back_heads[w]), device_id_type=mesh_id)

        @pl.when(gets_back[w])
        def _():
            pl.semaphore_signal(barrier, 1, device_id=device(block + distance, back_heads[w]), device_id_type=mesh_id)

    peers = len(partners)
    for w in range(WIN):
        peers = peers + sends_back[w].astype(jnp.int32) + gets_back[w].astype(jnp.int32)
    pl.semaphore_wait(barrier, peers)

    windows = x_ref.shape[0]
    kept = [x_ref, a1, a2]
    outgoing = [None, t1, t2]
    targets = [r1, r2, r3]
    copies = [[None] * windows for _ in range(3)]

    def keep_bit(stage, w):
        if stage > 0 and w == WIN - 1:
            return 1 - bits[stage]
        return bits[stage]

    def send(stage, w):
        keep = keep_bit(stage, w)
        source = x_ref.at[w, 1 - keep] if stage == 0 else outgoing[stage].at[w]
        copy = pltpu.make_async_remote_copy(
            src_ref=source,
            dst_ref=targets[stage].at[w],
            send_sem=sends.at[stage, w],
            recv_sem=recvs.at[stage, w],
            device_id=(dcn, blk, partners[stage]),
            device_id_type=mesh_id,
        )
        copy.start()
        copies[stage][w] = copy

    def back_copy(w, b):
        return pltpu.make_async_remote_copy(
            src_ref=a3.at[w],
            dst_ref=back.at[w],
            send_sem=sends.at[3, w],
            recv_sem=recvs.at[3, w],
            device_id=device(b, back_heads[w]),
            device_id_type=mesh_id,
        )

    for w in range(windows):
        send(0, w)
    for stage in range(3):
        for w in range(windows):
            copies[stage][w].wait_recv()
            arrived = targets[stage][w].astype(jnp.float32)
            summed = kept[stage][w, keep_bit(stage, w)] + arrived
            if stage < 2:
                kept[stage + 1][w] = summed
                away = kept[stage + 1][w, 1 - keep_bit(stage + 1, w)]
                outgoing[stage + 1][w] = away.astype(outgoing[stage + 1].dtype)
                send(stage + 1, w)
            elif w < WIN:
                a3[w] = summed.astype(a3.dtype)

                @pl.when(sends_back[w])
                def _():
                    back_copy(w, block - (WIN - w)).start()

            else:
                total[...] = summed
    for w in range(WIN - 1, -1, -1):

        @pl.when(gets_back[w])
        def _():
            back_copy(w, block + WIN - w).wait_recv()
            total[...] = total[...] + back[w].astype(jnp.float32)

    width = k_out.shape[1]
    k_out[...] = total[:, :width].astype(k_out.dtype)
    v_out[...] = total[:, width:].astype(v_out.dtype)
    for stage in range(3):
        for w in range(windows):
            copies[stage][w].wait_send()
    for w in range(WIN):

        @pl.when(sends_back[w])
        def _():
            back_copy(w, block - (WIN - w)).wait_send()


def grad_reduce(chunks, width, dtype):
    windows, rest = chunks.shape[0], chunks.shape[4:]
    f32 = jnp.float32
    link = jnp.bfloat16
    out = jax.ShapeDtypeStruct((rest[0], width), dtype)
    return pl.pallas_call(
        grad_reduce_kernel,
        out_shape=(out, out),
        in_specs=[pl.BlockSpec(memory_space=pltpu.VMEM)],
        out_specs=(pl.BlockSpec(memory_space=pltpu.VMEM), pl.BlockSpec(memory_space=pltpu.VMEM)),
        scratch_shapes=[
            pltpu.VMEM((windows, 2, 2) + rest, f32),
            pltpu.VMEM((windows, 2) + rest, link),
            pltpu.VMEM((windows,) + rest, link),
            pltpu.VMEM((windows, 2, 2) + rest, f32),
            pltpu.VMEM((windows, 2) + rest, f32),
            pltpu.VMEM((windows, 2) + rest, link),
            pltpu.VMEM((windows,) + rest, link),
            pltpu.VMEM((WIN,) + rest, link),
            pltpu.VMEM(rest, f32),
            pltpu.VMEM((WIN,) + rest, link),
            pltpu.SemaphoreType.DMA((4, windows)),
            pltpu.SemaphoreType.DMA((4, windows)),
        ],
        compiler_params=pltpu.CompilerParams(collective_id=0, has_side_effects=True),
    )(chunks)


def attention_kernel(q_ref, d_ref, k_ref, v_ref, s_ref, dq_ref, t_ref, dk_acc, dv_acc):
    heads, rows, width = q_ref.shape
    span = k_ref.shape[0]
    tile = 128
    reach = min(span, WIN * rows + tile)
    scale = width ** (-0.5)
    f32 = jnp.float32
    dk_acc[...] = jnp.zeros_like(dk_acc)
    dv_acc[...] = jnp.zeros_like(dv_acc)
    contract_last = (((1,), (1,)), ((), ()))
    contract_first = (((0,), (0,)), ((), ()))
    for h in range(heads):
        for r0 in range(0, rows, tile):
            k0 = min(r0, span - reach)
            qt = q_ref[h, r0 : r0 + tile, :]
            dt = d_ref[h, r0 : r0 + tile, :]
            kt = k_ref[k0 : k0 + reach, :]
            vt = v_ref[k0 : k0 + reach, :]
            starts = s_ref[r0 : r0 + tile, :]
            row = r0 + lax.broadcasted_iota(jnp.int32, (tile, reach), 0)
            col = k0 + lax.broadcasted_iota(jnp.int32, (tile, reach), 1)
            visible = (col >= starts) & (col <= row + WIN * rows)
            scores = lax.dot_general(qt, kt, contract_last, preferred_element_type=f32) * scale
            top = jnp.max(jnp.where(visible, scores, -1e30), axis=1, keepdims=True)
            expo = jnp.where(visible, jnp.exp(scores - top), 0.0)
            lse = top + jnp.log(jnp.sum(expo, axis=1, keepdims=True))
            prob = jnp.where(visible, jnp.exp(scores - lse), 0.0)
            prob_low = prob.astype(jnp.bfloat16)
            attended = jnp.dot(prob_low, vt, preferred_element_type=f32)
            delta = jnp.sum(dt.astype(f32) * attended, axis=1, keepdims=True)
            dprob = lax.dot_general(dt, vt, contract_last, preferred_element_type=f32)
            dscore = (prob * (dprob - delta)).astype(jnp.bfloat16)
            dq = jnp.dot(dscore, kt, preferred_element_type=f32) * scale
            dq_ref[h, r0 : r0 + tile, :] = dq.astype(dq_ref.dtype)
            dk_acc[k0 : k0 + reach, :] += lax.dot_general(dscore, qt, contract_first, preferred_element_type=f32)
            dv_acc[k0 : k0 + reach, :] += lax.dot_general(prob_low, dt, contract_first, preferred_element_type=f32)
    piece = t_ref.shape[4]
    for w in range(t_ref.shape[0]):
        for c in range(rows // piece):
            first = w * rows + c * piece
            place = (w, c % 2, (c // 2) % 2, c // 4)
            t_ref[place + (slice(None), slice(0, width))] = dk_acc[first : first + piece, :] * scale
            t_ref[place + (slice(None), slice(width, 2 * width))] = dv_acc[first : first + piece, :]


def attention(q, dout, kwin, vwin, starts, parts):
    heads, rows, width = q.shape
    span = kwin.shape[0]
    f32 = jnp.float32
    piece = rows // parts
    vmem = pl.BlockSpec(memory_space=pltpu.VMEM)
    return pl.pallas_call(
        attention_kernel,
        out_shape=(
            jax.ShapeDtypeStruct(q.shape, q.dtype),
            jax.ShapeDtypeStruct((span // rows, 2, 2, 2, piece, 2 * width), f32),
        ),
        in_specs=[vmem] * 5,
        out_specs=(vmem, vmem),
        scratch_shapes=[pltpu.VMEM((span, width), f32), pltpu.VMEM((span, width), f32)],
    )(q, dout, kwin, vwin, starts)


def local_grads(q, dout, starts, kwin, value_window, qpos, kpos):
    scale = q.shape[-1] ** (-0.5)
    visible = (kpos[None, :] >= starts[:, None]) & (kpos[None, :] <= qpos[:, None])
    scores = jnp.einsum("ihe,je->hij", q, kwin, preferred_element_type=jnp.float32) * scale
    top = jnp.max(jnp.where(visible[None], scores, -1e30), axis=-1, keepdims=True)
    expo = jnp.where(visible[None], jnp.exp(scores - top), 0.0)
    lse = top + jnp.log(jnp.sum(expo, axis=-1, keepdims=True))
    prob = jnp.where(visible[None], jnp.exp(scores - lse), 0.0)
    prob_low = prob.astype(jnp.bfloat16)
    attended_keys = jnp.einsum(
        "hij,je->ihe", prob_low, value_window, preferred_element_type=jnp.float32
    )
    delta = jnp.sum(dout.astype(jnp.float32) * attended_keys, axis=-1)
    dprob = jnp.einsum("ihe,je->hij", dout, value_window, preferred_element_type=jnp.float32)
    dscore = (prob * (dprob - jnp.transpose(delta)[:, :, None])).astype(jnp.bfloat16)
    dq = (
        jnp.einsum("hij,je->ihe", dscore, kwin, preferred_element_type=jnp.float32) * scale
    ).astype(jnp.bfloat16)
    dk = jnp.einsum("hij,ihe->je", dscore, q, preferred_element_type=jnp.float32) * scale
    dv = jnp.einsum("hij,ihe->je", prob_low, dout, preferred_element_type=jnp.float32)
    return (dq, jnp.concatenate([dk, dv], axis=1))


def body(queries, keys, values, out_grad, doc_start):
    rows = keys.shape[0]
    window_width = keys.shape[1]
    local_heads = queries.shape[1]
    position = lax.axis_index(("dcn", "blk"))
    packed = jnp.stack([keys, values])
    pieces = []
    for step in range(WIN, 0, -1):
        if step == 1:
            pieces.append(nearest_next(packed))
        else:
            pieces.append(from_behind(packed, ("dcn", "blk"), step))
    pieces.append(packed)
    window = jnp.concatenate(pieces, axis=1)
    window_span = (WIN + 1) * rows
    first_position = position * rows
    qpos = first_position + jnp.arange(rows, dtype=jnp.int32)
    kpos = first_position - WIN * rows + jnp.arange(window_span, dtype=jnp.int32)
    parts = lax.axis_size("head")
    window_start = first_position - WIN * rows
    starts = (doc_start - window_start).reshape(rows, 1)
    dq, chunks = attention(
        jnp.transpose(queries, (1, 0, 2)),
        jnp.transpose(out_grad, (1, 0, 2)),
        window[0],
        window[1],
        starts,
        parts,
    )
    q_grad = jnp.transpose(dq, (1, 0, 2))
    k_grad, v_grad = grad_reduce(chunks, window_width, jnp.bfloat16)
    return (q_grad, k_grad, v_grad)


def solution(mesh):
    in_specs = (
        P(("dcn", "blk"), "head", None),
        P(("dcn", "blk"), None),
        P(("dcn", "blk"), None),
        P(("dcn", "blk"), "head", None),
        P(("dcn", "blk")),
    )
    out_specs = (
        P(("dcn", "blk"), "head", None),
        P(("dcn", "blk", "head"), None),
        P(("dcn", "blk", "head"), None),
    )
    return jax.shard_map(body, mesh=mesh, in_specs=in_specs, out_specs=out_specs, check_vma=False)
```

```python
import jax
import jax.numpy as jnp
from jax import lax
from jax.sharding import PartitionSpec as P
from jax.experimental import pallas as pl
from jax.experimental.pallas import tpu as pltpu

WIN = 2


def from_behind(block, axis, distance):
    devices = range(lax.axis_size(axis))
    route = [(i - distance, i) for i in devices if i - distance in devices]
    return lax.ppermute(block, axis, route)


def mirror(head, parts):
    lanes = parts // 2
    return (lanes - 1 - head // 2) * 2 + head % 2


def nearest_next(block, back=False):
    parts = lax.axis_size("head")
    blocks = lax.axis_size(("dcn", "blk"))
    route = []
    for b in range(blocks - 1):
        for h in range(parts):
            pair = (b * parts + h, (b + 1) * parts + mirror(h, parts))
            route.append(pair[::-1] if back else pair)
    return lax.ppermute(block, ("dcn", "blk", "head"), route)


def grad_reduce_kernel(x_ref, o_ref, r1, r2, r3, a1, a2, t1, t2, a3, total, back, sends, recvs):
    mesh_id = pl.DeviceIdType.MESH
    dcn = lax.axis_index("dcn")
    blk = lax.axis_index("blk")
    head = lax.axis_index("head")
    per_dcn = lax.axis_size("blk")
    blocks = lax.axis_size("dcn") * per_dcn
    parts = lax.axis_size("head")
    block = dcn * per_dcn + blk
    bits = [head % 2, (head // 2) % 2, (head // 4) % 2]
    partners = [head + 1 - 2 * bits[0], head + 2 - 4 * bits[1], head + 4 - 8 * bits[2]]
    flipped = mirror(head, parts)

    def device(b, h):
        return (b // per_dcn, b % per_dcn, h)

    back_heads = [flipped if w == WIN - 1 else head for w in range(WIN)]
    sends_back = [block >= WIN - w for w in range(WIN)]
    gets_back = [block + WIN - w < blocks for w in range(WIN)]
    barrier = pltpu.get_barrier_semaphore()
    for partner in partners:
        pl.semaphore_signal(barrier, 1, device_id=(dcn, blk, partner), device_id_type=mesh_id)
    for w in range(WIN):
        distance = WIN - w

        @pl.when(sends_back[w])
        def _():
            pl.semaphore_signal(barrier, 1, device_id=device(block - distance, back_heads[w]), device_id_type=mesh_id)

        @pl.when(gets_back[w])
        def _():
            pl.semaphore_signal(barrier, 1, device_id=device(block + distance, back_heads[w]), device_id_type=mesh_id)

    peers = len(partners)
    for w in range(WIN):
        peers = peers + sends_back[w].astype(jnp.int32) + gets_back[w].astype(jnp.int32)
    pl.semaphore_wait(barrier, peers)

    windows = x_ref.shape[0]
    kept = [x_ref, a1, a2]
    outgoing = [None, t1, t2]
    targets = [r1, r2, r3]
    copies = [[None] * windows for _ in range(3)]

    def keep_bit(stage, w):
        if stage > 0 and w == WIN - 1:
            return 1 - bits[stage]
        return bits[stage]

    def send(stage, w):
        keep = keep_bit(stage, w)
        source = x_ref.at[w, 1 - keep] if stage == 0 else outgoing[stage].at[w]
        copy = pltpu.make_async_remote_copy(
            src_ref=source,
            dst_ref=targets[stage].at[w],
            send_sem=sends.at[stage, w],
            recv_sem=recvs.at[stage, w],
            device_id=(dcn, blk, partners[stage]),
            device_id_type=mesh_id,
        )
        copy.start()
        copies[stage][w] = copy

    def back_copy(w, b):
        return pltpu.make_async_remote_copy(
            src_ref=a3.at[w],
            dst_ref=back.at[w],
            send_sem=sends.at[3, w],
            recv_sem=recvs.at[3, w],
            device_id=device(b, back_heads[w]),
            device_id_type=mesh_id,
        )

    for w in range(windows):
        send(0, w)
    for stage in range(3):
        for w in range(windows):
            copies[stage][w].wait_recv()
            arrived = targets[stage][w].astype(jnp.float32)
            summed = kept[stage][w, keep_bit(stage, w)] + arrived
            if stage < 2:
                kept[stage + 1][w] = summed
                away = kept[stage + 1][w, 1 - keep_bit(stage + 1, w)]
                outgoing[stage + 1][w] = away.astype(outgoing[stage + 1].dtype)
                send(stage + 1, w)
            elif w < WIN:
                a3[w] = summed.astype(a3.dtype)

                @pl.when(sends_back[w])
                def _():
                    back_copy(w, block - (WIN - w)).start()

            else:
                total[...] = summed
    for w in range(WIN - 1, -1, -1):

        @pl.when(gets_back[w])
        def _():
            back_copy(w, block + WIN - w).wait_recv()
            total[...] = total[...] + back[w].astype(jnp.float32)

    o_ref[...] = total[...]
    for stage in range(3):
        for w in range(windows):
            copies[stage][w].wait_send()
    for w in range(WIN):

        @pl.when(sends_back[w])
        def _():
            back_copy(w, block - (WIN - w)).wait_send()


def grad_reduce(chunks, width, dtype):
    windows, rest = chunks.shape[0], chunks.shape[4:]
    f32 = jnp.float32
    link = jnp.bfloat16
    total = pl.pallas_call(
        grad_reduce_kernel,
        out_shape=jax.ShapeDtypeStruct(rest, f32),
        in_specs=[pl.BlockSpec(memory_space=pltpu.VMEM)],
        out_specs=pl.BlockSpec(memory_space=pltpu.VMEM),
        scratch_shapes=[
            pltpu.VMEM((windows, 2, 2) + rest, f32),
            pltpu.VMEM((windows, 2) + rest, link),
            pltpu.VMEM((windows,) + rest, link),
            pltpu.VMEM((windows, 2, 2) + rest, f32),
            pltpu.VMEM((windows, 2) + rest, f32),
            pltpu.VMEM((windows, 2) + rest, link),
            pltpu.VMEM((windows,) + rest, link),
            pltpu.VMEM((WIN,) + rest, link),
            pltpu.VMEM(rest, f32),
            pltpu.VMEM((WIN,) + rest, link),
            pltpu.SemaphoreType.DMA((4, windows)),
            pltpu.SemaphoreType.DMA((4, windows)),
        ],
        compiler_params=pltpu.CompilerParams(collective_id=0, has_side_effects=True),
    )(chunks)
    return total[:, :width].astype(dtype), total[:, width:].astype(dtype)


def attention_kernel(q_ref, d_ref, w_ref, s_ref, dq_ref, t_ref, dk_acc, dv_acc):
    heads, rows, width = q_ref.shape
    span = w_ref.shape[1]
    tile = 128
    reach = min(span, WIN * rows + tile)
    scale = width ** (-0.5)
    f32 = jnp.float32
    dk_acc[...] = jnp.zeros_like(dk_acc)
    dv_acc[...] = jnp.zeros_like(dv_acc)
    contract_last = (((1,), (1,)), ((), ()))
    contract_first = (((0,), (0,)), ((), ()))
    for h in range(heads):
        for r0 in range(0, rows, tile):
            k0 = min(r0, span - reach)
            qt = q_ref[h, r0 : r0 + tile, :]
            dt = d_ref[h, r0 : r0 + tile, :]
            kt = w_ref[0, k0 : k0 + reach, :]
            vt = w_ref[1, k0 : k0 + reach, :]
            starts = s_ref[r0 : r0 + tile, :]
            row = r0 + lax.broadcasted_iota(jnp.int32, (tile, reach), 0)
            col = k0 + lax.broadcasted_iota(jnp.int32, (tile, reach), 1)
            visible = (col >= starts) & (col <= row + WIN * rows)
            scores = lax.dot_general(qt, kt, contract_last, preferred_element_type=f32) * scale
            top = jnp.max(jnp.where(visible, scores, -1e30), axis=1, keepdims=True)
            expo = jnp.where(visible, jnp.exp(scores - top), 0.0)
            prob = expo / jnp.sum(expo, axis=1, keepdims=True)
            prob_low = prob.astype(jnp.bfloat16)
            attended = jnp.dot(prob_low, vt, preferred_element_type=f32)
            delta = jnp.sum(dt.astype(f32) * attended, axis=1, keepdims=True)
            dprob = lax.dot_general(dt, vt, contract_last, preferred_element_type=f32)
            dscore = (prob * (dprob - delta)).astype(jnp.bfloat16)
            dq = jnp.dot(dscore, kt, preferred_element_type=f32) * scale
            dq_ref[h, r0 : r0 + tile, :] = dq.astype(dq_ref.dtype)
            dk_acc[k0 : k0 + reach, :] += lax.dot_general(dscore, qt, contract_first, preferred_element_type=f32)
            dv_acc[k0 : k0 + reach, :] += lax.dot_general(prob_low, dt, contract_first, preferred_element_type=f32)
    piece = t_ref.shape[4]
    for w in range(t_ref.shape[0]):
        for c in range(rows // piece):
            first = w * rows + c * piece
            place = (w, c % 2, (c // 2) % 2, c // 4)
            t_ref[place + (slice(None), slice(0, width))] = dk_acc[first : first + piece, :] * scale
            t_ref[place + (slice(None), slice(width, 2 * width))] = dv_acc[first : first + piece, :]


def attention(q, dout, window, starts, parts):
    heads, rows, width = q.shape
    span = window.shape[1]
    f32 = jnp.float32
    piece = rows // parts
    vmem = pl.BlockSpec(memory_space=pltpu.VMEM)
    return pl.pallas_call(
        attention_kernel,
        out_shape=(
            jax.ShapeDtypeStruct(q.shape, q.dtype),
            jax.ShapeDtypeStruct((span // rows, 2, 2, 2, piece, 2 * width), f32),
        ),
        in_specs=[vmem] * 4,
        out_specs=(vmem, vmem),
        scratch_shapes=[pltpu.VMEM((span, width), f32), pltpu.VMEM((span, width), f32)],
    )(q, dout, window, starts)


def local_grads(q, dout, starts, kwin, value_window, qpos, kpos):
    scale = q.shape[-1] ** (-0.5)
    visible = (kpos[None, :] >= starts[:, None]) & (kpos[None, :] <= qpos[:, None])
    scores = jnp.einsum("ihe,je->hij", q, kwin, preferred_element_type=jnp.float32) * scale
    top = jnp.max(jnp.where(visible[None], scores, -1e30), axis=-1, keepdims=True)
    expo = jnp.where(visible[None], jnp.exp(scores - top), 0.0)
    lse = top + jnp.log(jnp.sum(expo, axis=-1, keepdims=True))
    prob = jnp.where(visible[None], jnp.exp(scores - lse), 0.0)
    prob_low = prob.astype(jnp.bfloat16)
    attended_keys = jnp.einsum(
        "hij,je->ihe", prob_low, value_window, preferred_element_type=jnp.float32
    )
    delta = jnp.sum(dout.astype(jnp.float32) * attended_keys, axis=-1)
    dprob = jnp.einsum("ihe,je->hij", dout, value_window, preferred_element_type=jnp.float32)
    dscore = (prob * (dprob - jnp.transpose(delta)[:, :, None])).astype(jnp.bfloat16)
    dq = (
        jnp.einsum("hij,je->ihe", dscore, kwin, preferred_element_type=jnp.float32) * scale
    ).astype(jnp.bfloat16)
    dk = jnp.einsum("hij,ihe->je", dscore, q, preferred_element_type=jnp.float32) * scale
    dv = jnp.einsum("hij,ihe->je", prob_low, dout, preferred_element_type=jnp.float32)
    return (dq, jnp.concatenate([dk, dv], axis=1))


def body(queries, keys, values, out_grad, doc_start):
    rows = keys.shape[0]
    window_width = keys.shape[1]
    local_heads = queries.shape[1]
    position = lax.axis_index(("dcn", "blk"))
    packed = jnp.stack([keys, values])
    pieces = []
    for step in range(WIN, 0, -1):
        if step == 1:
            pieces.append(nearest_next(packed))
        else:
            pieces.append(from_behind(packed, ("dcn", "blk"), step))
    pieces.append(packed)
    window = jnp.concatenate(pieces, axis=1)
    window_span = (WIN + 1) * rows
    first_position = position * rows
    qpos = first_position + jnp.arange(rows, dtype=jnp.int32)
    kpos = first_position - WIN * rows + jnp.arange(window_span, dtype=jnp.int32)
    parts = lax.axis_size("head")
    window_start = first_position - WIN * rows
    starts = (doc_start - window_start).reshape(rows, 1)
    dq, chunks = attention(
        jnp.transpose(queries, (1, 0, 2)),
        jnp.transpose(out_grad, (1, 0, 2)),
        window,
        starts,
        parts,
    )
    q_grad = jnp.transpose(dq, (1, 0, 2))
    k_grad, v_grad = grad_reduce(chunks, window_width, jnp.bfloat16)
    return (q_grad, k_grad, v_grad)


def solution(mesh):
    in_specs = (
        P(("dcn", "blk"), "head", None),
        P(("dcn", "blk"), None),
        P(("dcn", "blk"), None),
        P(("dcn", "blk"), "head", None),
        P(("dcn", "blk")),
    )
    out_specs = (
        P(("dcn", "blk"), "head", None),
        P(("dcn", "blk", "head"), None),
        P(("dcn", "blk", "head"), None),
    )
    return jax.shard_map(body, mesh=mesh, in_specs=in_specs, out_specs=out_specs, check_vma=False)
```

```python
import jax
import jax.numpy as jnp
from jax import lax
from jax.sharding import PartitionSpec as P
from jax.experimental import pallas as pl
from jax.experimental.pallas import tpu as pltpu

WIN = 2


def from_behind(block, axis, distance):
    devices = range(lax.axis_size(axis))
    route = [(i - distance, i) for i in devices if i - distance in devices]
    return lax.ppermute(block, axis, route)


def mirror(head, parts):
    lanes = parts // 2
    return (lanes - 1 - head // 2) * 2 + head % 2


def nearest_next(block, back=False):
    parts = lax.axis_size("head")
    blocks = lax.axis_size(("dcn", "blk"))
    route = []
    for b in range(blocks - 1):
        for h in range(parts):
            pair = (b * parts + h, (b + 1) * parts + mirror(h, parts))
            route.append(pair[::-1] if back else pair)
    return lax.ppermute(block, ("dcn", "blk", "head"), route)


def grad_reduce_kernel(x_ref, o_ref, r1, r2, r3, a1, a2, t1, t2, a3, total, back, sends, recvs):
    mesh_id = pl.DeviceIdType.MESH
    dcn = lax.axis_index("dcn")
    blk = lax.axis_index("blk")
    head = lax.axis_index("head")
    per_dcn = lax.axis_size("blk")
    blocks = lax.axis_size("dcn") * per_dcn
    parts = lax.axis_size("head")
    block = dcn * per_dcn + blk
    bits = [head % 2, (head // 2) % 2, (head // 4) % 2]
    partners = [head + 1 - 2 * bits[0], head + 2 - 4 * bits[1], head + 4 - 8 * bits[2]]
    flipped = mirror(head, parts)

    def device(b, h):
        return (b // per_dcn, b % per_dcn, h)

    back_heads = [flipped if w == WIN - 1 else head for w in range(WIN)]
    sends_back = [block >= WIN - w for w in range(WIN)]
    gets_back = [block + WIN - w < blocks for w in range(WIN)]
    barrier = pltpu.get_barrier_semaphore()
    for partner in partners:
        pl.semaphore_signal(barrier, 1, device_id=(dcn, blk, partner), device_id_type=mesh_id)
    for w in range(WIN):
        distance = WIN - w

        @pl.when(sends_back[w])
        def _():
            pl.semaphore_signal(barrier, 1, device_id=device(block - distance, back_heads[w]), device_id_type=mesh_id)

        @pl.when(gets_back[w])
        def _():
            pl.semaphore_signal(barrier, 1, device_id=device(block + distance, back_heads[w]), device_id_type=mesh_id)

    peers = len(partners)
    for w in range(WIN):
        peers = peers + sends_back[w].astype(jnp.int32) + gets_back[w].astype(jnp.int32)
    pl.semaphore_wait(barrier, peers)

    windows = x_ref.shape[0]
    kept = [x_ref, a1, a2]
    outgoing = [None, t1, t2]
    targets = [r1, r2, r3]
    copies = [[None] * windows for _ in range(3)]

    def keep_bit(stage, w):
        if stage > 0 and w == WIN - 1:
            return 1 - bits[stage]
        return bits[stage]

    def send(stage, w):
        keep = keep_bit(stage, w)
        source = x_ref.at[w, 1 - keep] if stage == 0 else outgoing[stage].at[w]
        copy = pltpu.make_async_remote_copy(
            src_ref=source,
            dst_ref=targets[stage].at[w],
            send_sem=sends.at[stage, w],
            recv_sem=recvs.at[stage, w],
            device_id=(dcn, blk, partners[stage]),
            device_id_type=mesh_id,
        )
        copy.start()
        copies[stage][w] = copy

    def back_copy(w, b):
        return pltpu.make_async_remote_copy(
            src_ref=a3.at[w],
            dst_ref=back.at[w],
            send_sem=sends.at[3, w],
            recv_sem=recvs.at[3, w],
            device_id=device(b, back_heads[w]),
            device_id_type=mesh_id,
        )

    for w in range(windows):
        send(0, w)
    for stage in range(3):
        for w in range(windows):
            copies[stage][w].wait_recv()
            arrived = targets[stage][w].astype(jnp.float32)
            summed = kept[stage][w, keep_bit(stage, w)] + arrived
            if stage < 2:
                kept[stage + 1][w] = summed
                away = kept[stage + 1][w, 1 - keep_bit(stage + 1, w)]
                outgoing[stage + 1][w] = away.astype(outgoing[stage + 1].dtype)
                send(stage + 1, w)
            elif w < WIN:
                a3[w] = summed.astype(a3.dtype)

                @pl.when(sends_back[w])
                def _():
                    back_copy(w, block - (WIN - w)).start()

            else:
                total[...] = summed
    for w in range(WIN - 1, -1, -1):

        @pl.when(gets_back[w])
        def _():
            back_copy(w, block + WIN - w).wait_recv()
            total[...] = total[...] + back[w].astype(jnp.float32)

    o_ref[...] = total[...]
    for stage in range(3):
        for w in range(windows):
            copies[stage][w].wait_send()
    for w in range(WIN):

        @pl.when(sends_back[w])
        def _():
            back_copy(w, block - (WIN - w)).wait_send()


def grad_reduce(chunks, width, dtype):
    windows, rest = chunks.shape[0], chunks.shape[4:]
    f32 = jnp.float32
    link = jnp.bfloat16
    total = pl.pallas_call(
        grad_reduce_kernel,
        out_shape=jax.ShapeDtypeStruct(rest, f32),
        in_specs=[pl.BlockSpec(memory_space=pltpu.VMEM)],
        out_specs=pl.BlockSpec(memory_space=pltpu.VMEM),
        scratch_shapes=[
            pltpu.VMEM((windows, 2, 2) + rest, f32),
            pltpu.VMEM((windows, 2) + rest, link),
            pltpu.VMEM((windows,) + rest, link),
            pltpu.VMEM((windows, 2, 2) + rest, f32),
            pltpu.VMEM((windows, 2) + rest, f32),
            pltpu.VMEM((windows, 2) + rest, link),
            pltpu.VMEM((windows,) + rest, link),
            pltpu.VMEM((WIN,) + rest, link),
            pltpu.VMEM(rest, f32),
            pltpu.VMEM((WIN,) + rest, link),
            pltpu.SemaphoreType.DMA((4, windows)),
            pltpu.SemaphoreType.DMA((4, windows)),
        ],
        compiler_params=pltpu.CompilerParams(collective_id=0, has_side_effects=True),
    )(chunks)
    return total[:, :width].astype(dtype), total[:, width:].astype(dtype)


def attention_kernel(f_ref, q_ref, d_ref, w_ref, s_ref, dq_ref, t_ref, dk_acc, dv_acc):
    heads, rows, width = q_ref.shape
    span = w_ref.shape[1]
    tile = 128
    reach = min(span, WIN * rows + tile)
    skip = rows
    scale = width ** (-0.5)
    f32 = jnp.float32
    dk_acc[...] = jnp.zeros_like(dk_acc)
    dv_acc[...] = jnp.zeros_like(dv_acc)
    contract_last = (((1,), (1,)), ((), ()))
    contract_first = (((0,), (0,)), ((), ()))

    def tile_grads(h, r0, k0, size):
        qt = q_ref[h, r0 : r0 + tile, :]
        dt = d_ref[h, r0 : r0 + tile, :]
        kt = w_ref[0, k0 : k0 + size, :]
        vt = w_ref[1, k0 : k0 + size, :]
        starts = s_ref[r0 : r0 + tile, :]
        row = r0 + lax.broadcasted_iota(jnp.int32, (tile, size), 0)
        col = k0 + lax.broadcasted_iota(jnp.int32, (tile, size), 1)
        visible = (col >= starts) & (col <= row + WIN * rows)
        scores = lax.dot_general(qt, kt, contract_last, preferred_element_type=f32) * scale
        top = jnp.max(jnp.where(visible, scores, -1e30), axis=1, keepdims=True)
        expo = jnp.where(visible, jnp.exp(scores - top), 0.0)
        prob = expo / jnp.sum(expo, axis=1, keepdims=True)
        prob_low = prob.astype(jnp.bfloat16)
        attended = jnp.dot(prob_low, vt, preferred_element_type=f32)
        delta = jnp.sum(dt.astype(f32) * attended, axis=1, keepdims=True)
        dprob = lax.dot_general(dt, vt, contract_last, preferred_element_type=f32)
        dscore = (prob * (dprob - delta)).astype(jnp.bfloat16)
        dq = jnp.dot(dscore, kt, preferred_element_type=f32) * scale
        dq_ref[h, r0 : r0 + tile, :] = dq.astype(dq_ref.dtype)
        dk_acc[k0 : k0 + size, :] += lax.dot_general(dscore, qt, contract_first, preferred_element_type=f32)
        dv_acc[k0 : k0 + size, :] += lax.dot_general(prob_low, dt, contract_first, preferred_element_type=f32)

    for h in range(heads):
        for t, r0 in enumerate(range(0, rows, tile)):
            k0 = min(r0, span - reach)
            short = f_ref[t] == 1

            @pl.when(short)
            def _():
                tile_grads(h, r0, k0 + skip, reach - skip)

            @pl.when(jnp.logical_not(short))
            def _():
                tile_grads(h, r0, k0, reach)

    piece = t_ref.shape[4]
    for w in range(t_ref.shape[0]):
        for c in range(rows // piece):
            first = w * rows + c * piece
            place = (w, c % 2, (c // 2) % 2, c // 4)
            t_ref[place + (slice(None), slice(0, width))] = dk_acc[first : first + piece, :] * scale
            t_ref[place + (slice(None), slice(width, 2 * width))] = dv_acc[first : first + piece, :]


def attention(q, dout, window, starts, parts):
    heads, rows, width = q.shape
    span = window.shape[1]
    f32 = jnp.float32
    piece = rows // parts
    tile = 128
    reach = min(span, WIN * rows + tile)
    firsts = jnp.arange(0, rows, tile, dtype=jnp.int32)
    lowest = jnp.minimum(firsts, span - reach)
    flags = (starts[firsts, 0] >= lowest + rows).astype(jnp.int32)
    vmem = pl.BlockSpec(memory_space=pltpu.VMEM)
    return pl.pallas_call(
        attention_kernel,
        out_shape=(
            jax.ShapeDtypeStruct(q.shape, q.dtype),
            jax.ShapeDtypeStruct((span // rows, 2, 2, 2, piece, 2 * width), f32),
        ),
        in_specs=[pl.BlockSpec(memory_space=pltpu.SMEM)] + [vmem] * 4,
        out_specs=(vmem, vmem),
        scratch_shapes=[pltpu.VMEM((span, width), f32), pltpu.VMEM((span, width), f32)],
    )(flags, q, dout, window, starts)


def local_grads(q, dout, starts, kwin, value_window, qpos, kpos):
    scale = q.shape[-1] ** (-0.5)
    visible = (kpos[None, :] >= starts[:, None]) & (kpos[None, :] <= qpos[:, None])
    scores = jnp.einsum("ihe,je->hij", q, kwin, preferred_element_type=jnp.float32) * scale
    top = jnp.max(jnp.where(visible[None], scores, -1e30), axis=-1, keepdims=True)
    expo = jnp.where(visible[None], jnp.exp(scores - top), 0.0)
    lse = top + jnp.log(jnp.sum(expo, axis=-1, keepdims=True))
    prob = jnp.where(visible[None], jnp.exp(scores - lse), 0.0)
    prob_low = prob.astype(jnp.bfloat16)
    attended_keys = jnp.einsum(
        "hij,je->ihe", prob_low, value_window, preferred_element_type=jnp.float32
    )
    delta = jnp.sum(dout.astype(jnp.float32) * attended_keys, axis=-1)
    dprob = jnp.einsum("ihe,je->hij", dout, value_window, preferred_element_type=jnp.float32)
    dscore = (prob * (dprob - jnp.transpose(delta)[:, :, None])).astype(jnp.bfloat16)
    dq = (
        jnp.einsum("hij,je->ihe", dscore, kwin, preferred_element_type=jnp.float32) * scale
    ).astype(jnp.bfloat16)
    dk = jnp.einsum("hij,ihe->je", dscore, q, preferred_element_type=jnp.float32) * scale
    dv = jnp.einsum("hij,ihe->je", prob_low, dout, preferred_element_type=jnp.float32)
    return (dq, jnp.concatenate([dk, dv], axis=1))


def body(queries, keys, values, out_grad, doc_start):
    rows = keys.shape[0]
    window_width = keys.shape[1]
    local_heads = queries.shape[1]
    position = lax.axis_index(("dcn", "blk"))
    packed = jnp.stack([keys, values])
    pieces = []
    for step in range(WIN, 0, -1):
        if step == 1:
            pieces.append(nearest_next(packed))
        else:
            pieces.append(from_behind(packed, ("dcn", "blk"), step))
    pieces.append(packed)
    window = jnp.concatenate(pieces, axis=1)
    window_span = (WIN + 1) * rows
    first_position = position * rows
    qpos = first_position + jnp.arange(rows, dtype=jnp.int32)
    kpos = first_position - WIN * rows + jnp.arange(window_span, dtype=jnp.int32)
    parts = lax.axis_size("head")
    window_start = first_position - WIN * rows
    starts = (doc_start - window_start).reshape(rows, 1)
    dq, chunks = attention(
        jnp.transpose(queries, (1, 0, 2)),
        jnp.transpose(out_grad, (1, 0, 2)),
        window,
        starts,
        parts,
    )
    q_grad = jnp.transpose(dq, (1, 0, 2))
    k_grad, v_grad = grad_reduce(chunks, window_width, jnp.bfloat16)
    return (q_grad, k_grad, v_grad)


def solution(mesh):
    in_specs = (
        P(("dcn", "blk"), "head", None),
        P(("dcn", "blk"), None),
        P(("dcn", "blk"), None),
        P(("dcn", "blk"), "head", None),
        P(("dcn", "blk")),
    )
    out_specs = (
        P(("dcn", "blk"), "head", None),
        P(("dcn", "blk", "head"), None),
        P(("dcn", "blk", "head"), None),
    )
    return jax.shard_map(body, mesh=mesh, in_specs=in_specs, out_specs=out_specs, check_vma=False)
```

```python
import jax
import jax.numpy as jnp
from jax import lax
from jax.sharding import PartitionSpec as P
from jax.experimental import pallas as pl
from jax.experimental.pallas import tpu as pltpu

WIN = 2


def from_behind(block, axis, distance):
    devices = range(lax.axis_size(axis))
    route = [(i - distance, i) for i in devices if i - distance in devices]
    return lax.ppermute(block, axis, route)


def mirror(head, parts):
    lanes = parts // 2
    return (lanes - 1 - head // 2) * 2 + head % 2


def nearest_next(block, back=False):
    parts = lax.axis_size("head")
    blocks = lax.axis_size(("dcn", "blk"))
    route = []
    for b in range(blocks - 1):
        for h in range(parts):
            pair = (b * parts + h, (b + 1) * parts + mirror(h, parts))
            route.append(pair[::-1] if back else pair)
    return lax.ppermute(block, ("dcn", "blk", "head"), route)


def grad_reduce_kernel(x_ref, o_ref, r1, r2, r3, a1, a2, t1, t2, a3, total, back, sends, recvs):
    mesh_id = pl.DeviceIdType.MESH
    dcn = lax.axis_index("dcn")
    blk = lax.axis_index("blk")
    head = lax.axis_index("head")
    per_dcn = lax.axis_size("blk")
    blocks = lax.axis_size("dcn") * per_dcn
    parts = lax.axis_size("head")
    block = dcn * per_dcn + blk
    bits = [head % 2, (head // 2) % 2, (head // 4) % 2]
    partners = [head + 1 - 2 * bits[0], head + 2 - 4 * bits[1], head + 4 - 8 * bits[2]]
    flipped = mirror(head, parts)

    def device(b, h):
        return (b // per_dcn, b % per_dcn, h)

    back_heads = [flipped if w == WIN - 1 else head for w in range(WIN)]
    sends_back = [block >= WIN - w for w in range(WIN)]
    gets_back = [block + WIN - w < blocks for w in range(WIN)]
    barrier = pltpu.get_barrier_semaphore()
    for partner in partners:
        pl.semaphore_signal(barrier, 1, device_id=(dcn, blk, partner), device_id_type=mesh_id)
    for w in range(WIN):
        distance = WIN - w

        @pl.when(sends_back[w])
        def _():
            pl.semaphore_signal(barrier, 1, device_id=device(block - distance, back_heads[w]), device_id_type=mesh_id)

        @pl.when(gets_back[w])
        def _():
            pl.semaphore_signal(barrier, 1, device_id=device(block + distance, back_heads[w]), device_id_type=mesh_id)

    peers = len(partners)
    for w in range(WIN):
        peers = peers + sends_back[w].astype(jnp.int32) + gets_back[w].astype(jnp.int32)
    pl.semaphore_wait(barrier, peers)

    windows = x_ref.shape[0]
    kept = [x_ref, a1, a2]
    outgoing = [None, t1, t2]
    targets = [r1, r2, r3]
    copies = [[None] * windows for _ in range(3)]

    def keep_bit(stage, w):
        if stage > 0 and w == WIN - 1:
            return 1 - bits[stage]
        return bits[stage]

    def send(stage, w):
        keep = keep_bit(stage, w)
        source = x_ref.at[w, 1 - keep] if stage == 0 else outgoing[stage].at[w]
        copy = pltpu.make_async_remote_copy(
            src_ref=source,
            dst_ref=targets[stage].at[w],
            send_sem=sends.at[stage, w],
            recv_sem=recvs.at[stage, w],
            device_id=(dcn, blk, partners[stage]),
            device_id_type=mesh_id,
        )
        copy.start()
        copies[stage][w] = copy

    def back_copy(w, b):
        return pltpu.make_async_remote_copy(
            src_ref=a3.at[w],
            dst_ref=back.at[w],
            send_sem=sends.at[3, w],
            recv_sem=recvs.at[3, w],
            device_id=device(b, back_heads[w]),
            device_id_type=mesh_id,
        )

    for w in range(windows):
        send(0, w)
    for stage in range(3):
        for w in range(windows):
            copies[stage][w].wait_recv()
            arrived = targets[stage][w].astype(jnp.float32)
            summed = kept[stage][w, keep_bit(stage, w)].astype(jnp.float32) + arrived
            if stage < 2:
                kept[stage + 1][w] = summed
                away = kept[stage + 1][w, 1 - keep_bit(stage + 1, w)]
                outgoing[stage + 1][w] = away.astype(outgoing[stage + 1].dtype)
                send(stage + 1, w)
            elif w < WIN:
                a3[w] = summed.astype(a3.dtype)

                @pl.when(sends_back[w])
                def _():
                    back_copy(w, block - (WIN - w)).start()

            else:
                total[...] = summed
    for w in range(WIN - 1, -1, -1):

        @pl.when(gets_back[w])
        def _():
            back_copy(w, block + WIN - w).wait_recv()
            total[...] = total[...] + back[w].astype(jnp.float32)

    o_ref[...] = total[...]
    for stage in range(3):
        for w in range(windows):
            copies[stage][w].wait_send()
    for w in range(WIN):

        @pl.when(sends_back[w])
        def _():
            back_copy(w, block - (WIN - w)).wait_send()


def grad_reduce(chunks, width, dtype):
    windows, rest = chunks.shape[0], chunks.shape[4:]
    f32 = jnp.float32
    link = jnp.bfloat16
    total = pl.pallas_call(
        grad_reduce_kernel,
        out_shape=jax.ShapeDtypeStruct(rest, f32),
        in_specs=[pl.BlockSpec(memory_space=pltpu.VMEM)],
        out_specs=pl.BlockSpec(memory_space=pltpu.VMEM),
        scratch_shapes=[
            pltpu.VMEM((windows, 2, 2) + rest, link),
            pltpu.VMEM((windows, 2) + rest, link),
            pltpu.VMEM((windows,) + rest, link),
            pltpu.VMEM((windows, 2, 2) + rest, f32),
            pltpu.VMEM((windows, 2) + rest, f32),
            pltpu.VMEM((windows, 2) + rest, link),
            pltpu.VMEM((windows,) + rest, link),
            pltpu.VMEM((WIN,) + rest, link),
            pltpu.VMEM(rest, f32),
            pltpu.VMEM((WIN,) + rest, link),
            pltpu.SemaphoreType.DMA((4, windows)),
            pltpu.SemaphoreType.DMA((4, windows)),
        ],
        compiler_params=pltpu.CompilerParams(collective_id=0, has_side_effects=True),
    )(chunks)
    return total[:, :width].astype(dtype), total[:, width:].astype(dtype)


def attention_kernel(q_ref, d_ref, w_ref, s_ref, dq_ref, t_ref, dk_acc, dv_acc):
    heads, rows, width = q_ref.shape
    span = w_ref.shape[1]
    tile = 128
    reach = min(span, WIN * rows + tile)
    scale = width ** (-0.5)
    f32 = jnp.float32
    dk_acc[...] = jnp.zeros_like(dk_acc)
    dv_acc[...] = jnp.zeros_like(dv_acc)
    contract_last = (((1,), (1,)), ((), ()))
    contract_first = (((0,), (0,)), ((), ()))
    for h in range(heads):
        for r0 in range(0, rows, tile):
            k0 = min(r0, span - reach)
            qt = q_ref[h, r0 : r0 + tile, :]
            dt = d_ref[h, r0 : r0 + tile, :]
            kt = w_ref[0, k0 : k0 + reach, :]
            vt = w_ref[1, k0 : k0 + reach, :]
            starts = s_ref[r0 : r0 + tile, :]
            row = r0 + lax.broadcasted_iota(jnp.int32, (tile, reach), 0)
            col = k0 + lax.broadcasted_iota(jnp.int32, (tile, reach), 1)
            visible = (col >= starts) & (col <= row + WIN * rows)
            scores = lax.dot_general(qt, kt, contract_last, preferred_element_type=f32) * scale
            top = jnp.max(jnp.where(visible, scores, -1e30), axis=1, keepdims=True)
            expo = jnp.where(visible, jnp.exp(scores - top), 0.0)
            prob = expo / jnp.sum(expo, axis=1, keepdims=True)
            prob_low = prob.astype(jnp.bfloat16)
            attended = jnp.dot(prob_low, vt, preferred_element_type=f32)
            delta = jnp.sum(dt.astype(f32) * attended, axis=1, keepdims=True)
            dprob = lax.dot_general(dt, vt, contract_last, preferred_element_type=f32)
            dscore = (prob * (dprob - delta)).astype(jnp.bfloat16)
            dq = jnp.dot(dscore, kt, preferred_element_type=f32) * scale
            dq_ref[h, r0 : r0 + tile, :] = dq.astype(dq_ref.dtype)
            dk_acc[k0 : k0 + reach, :] += lax.dot_general(dscore, qt, contract_first, preferred_element_type=f32)
            dv_acc[k0 : k0 + reach, :] += lax.dot_general(prob_low, dt, contract_first, preferred_element_type=f32)
    piece = t_ref.shape[4]
    for w in range(t_ref.shape[0]):
        for c in range(rows // piece):
            first = w * rows + c * piece
            place = (w, c % 2, (c // 2) % 2, c // 4)
            dk = dk_acc[first : first + piece, :] * scale
            t_ref[place + (slice(None), slice(0, width))] = dk.astype(t_ref.dtype)
            t_ref[place + (slice(None), slice(width, 2 * width))] = dv_acc[first : first + piece, :].astype(t_ref.dtype)


def attention(q, dout, window, starts, parts):
    heads, rows, width = q.shape
    span = window.shape[1]
    f32 = jnp.float32
    piece = rows // parts
    vmem = pl.BlockSpec(memory_space=pltpu.VMEM)
    return pl.pallas_call(
        attention_kernel,
        out_shape=(
            jax.ShapeDtypeStruct(q.shape, q.dtype),
            jax.ShapeDtypeStruct((span // rows, 2, 2, 2, piece, 2 * width), jnp.bfloat16),
        ),
        in_specs=[vmem] * 4,
        out_specs=(vmem, vmem),
        scratch_shapes=[pltpu.VMEM((span, width), f32), pltpu.VMEM((span, width), f32)],
    )(q, dout, window, starts)


def local_grads(q, dout, starts, kwin, value_window, qpos, kpos):
    scale = q.shape[-1] ** (-0.5)
    visible = (kpos[None, :] >= starts[:, None]) & (kpos[None, :] <= qpos[:, None])
    scores = jnp.einsum("ihe,je->hij", q, kwin, preferred_element_type=jnp.float32) * scale
    top = jnp.max(jnp.where(visible[None], scores, -1e30), axis=-1, keepdims=True)
    expo = jnp.where(visible[None], jnp.exp(scores - top), 0.0)
    lse = top + jnp.log(jnp.sum(expo, axis=-1, keepdims=True))
    prob = jnp.where(visible[None], jnp.exp(scores - lse), 0.0)
    prob_low = prob.astype(jnp.bfloat16)
    attended_keys = jnp.einsum(
        "hij,je->ihe", prob_low, value_window, preferred_element_type=jnp.float32
    )
    delta = jnp.sum(dout.astype(jnp.float32) * attended_keys, axis=-1)
    dprob = jnp.einsum("ihe,je->hij", dout, value_window, preferred_element_type=jnp.float32)
    dscore = (prob * (dprob - jnp.transpose(delta)[:, :, None])).astype(jnp.bfloat16)
    dq = (
        jnp.einsum("hij,je->ihe", dscore, kwin, preferred_element_type=jnp.float32) * scale
    ).astype(jnp.bfloat16)
    dk = jnp.einsum("hij,ihe->je", dscore, q, preferred_element_type=jnp.float32) * scale
    dv = jnp.einsum("hij,ihe->je", prob_low, dout, preferred_element_type=jnp.float32)
    return (dq, jnp.concatenate([dk, dv], axis=1))


def body(queries, keys, values, out_grad, doc_start):
    rows = keys.shape[0]
    window_width = keys.shape[1]
    local_heads = queries.shape[1]
    position = lax.axis_index(("dcn", "blk"))
    packed = jnp.stack([keys, values])
    pieces = []
    for step in range(WIN, 0, -1):
        if step == 1:
            pieces.append(nearest_next(packed))
        else:
            pieces.append(from_behind(packed, ("dcn", "blk"), step))
    pieces.append(packed)
    window = jnp.concatenate(pieces, axis=1)
    window_span = (WIN + 1) * rows
    first_position = position * rows
    qpos = first_position + jnp.arange(rows, dtype=jnp.int32)
    kpos = first_position - WIN * rows + jnp.arange(window_span, dtype=jnp.int32)
    parts = lax.axis_size("head")
    window_start = first_position - WIN * rows
    starts = (doc_start - window_start).reshape(rows, 1)
    dq, chunks = attention(
        jnp.transpose(queries, (1, 0, 2)),
        jnp.transpose(out_grad, (1, 0, 2)),
        window,
        starts,
        parts,
    )
    q_grad = jnp.transpose(dq, (1, 0, 2))
    k_grad, v_grad = grad_reduce(chunks, window_width, jnp.bfloat16)
    return (q_grad, k_grad, v_grad)


def solution(mesh):
    in_specs = (
        P(("dcn", "blk"), "head", None),
        P(("dcn", "blk"), None),
        P(("dcn", "blk"), None),
        P(("dcn", "blk"), "head", None),
        P(("dcn", "blk")),
    )
    out_specs = (
        P(("dcn", "blk"), "head", None),
        P(("dcn", "blk", "head"), None),
        P(("dcn", "blk", "head"), None),
    )
    return jax.shard_map(body, mesh=mesh, in_specs=in_specs, out_specs=out_specs, check_vma=False)
```

```python
import jax
import jax.numpy as jnp
from jax import lax
from jax.sharding import PartitionSpec as P
from jax.experimental import pallas as pl
from jax.experimental.pallas import tpu as pltpu

WIN = 2


def from_behind(block, axis, distance):
    devices = range(lax.axis_size(axis))
    route = [(i - distance, i) for i in devices if i - distance in devices]
    return lax.ppermute(block, axis, route)


def mirror(head, parts):
    lanes = parts // 2
    return (lanes - 1 - head // 2) * 2 + head % 2


def nearest_next(block, back=False):
    parts = lax.axis_size("head")
    blocks = lax.axis_size(("dcn", "blk"))
    route = []
    for b in range(blocks - 1):
        for h in range(parts):
            pair = (b * parts + h, (b + 1) * parts + mirror(h, parts))
            route.append(pair[::-1] if back else pair)
    return lax.ppermute(block, ("dcn", "blk", "head"), route)


def grad_reduce_kernel(x_ref, o_ref, r1, r2, r3, a1, a2, t1, t2, a3, total, back, sends, recvs):
    mesh_id = pl.DeviceIdType.MESH
    dcn = lax.axis_index("dcn")
    blk = lax.axis_index("blk")
    head = lax.axis_index("head")
    per_dcn = lax.axis_size("blk")
    blocks = lax.axis_size("dcn") * per_dcn
    block = dcn * per_dcn + blk
    bits = [head % 2, (head // 2) % 2, (head // 4) % 2]
    partners = [head + 1 - 2 * bits[0], head + 2 - 4 * bits[1], head + 4 - 8 * bits[2]]

    def device(b, h):
        return (b // per_dcn, b % per_dcn, h)

    def keep_bit(stage, w):
        if stage > 0 and w == WIN - 1:
            return 1 - bits[stage]
        return bits[stage]

    def owner(w, half):
        return bits[0] + 2 * keep_bit(1, w) + 4 * half

    def sender(w, slot):
        second = bits[1] if w != WIN - 1 else 1 - bits[1]
        return bits[0] + 2 * second + 4 * slot

    sends_back = [block >= WIN - w for w in range(WIN)]
    gets_back = [block + WIN - w < blocks for w in range(WIN)]
    barrier = pltpu.get_barrier_semaphore()
    for partner in partners:
        pl.semaphore_signal(barrier, 1, device_id=(dcn, blk, partner), device_id_type=mesh_id)
    peers = len(partners)
    for w in range(WIN):
        distance = WIN - w
        for half in range(2):

            @pl.when(sends_back[w])
            def _():
                pl.semaphore_signal(barrier, 1, device_id=device(block - distance, owner(w, half)), device_id_type=mesh_id)

            @pl.when(gets_back[w])
            def _():
                pl.semaphore_signal(barrier, 1, device_id=device(block + distance, sender(w, half)), device_id_type=mesh_id)

        peers = peers + 2 * sends_back[w].astype(jnp.int32) + 2 * gets_back[w].astype(jnp.int32)
    pl.semaphore_wait(barrier, peers)

    windows = x_ref.shape[0]
    kept = [x_ref, a1, a2]
    outgoing = [None, t1, t2]
    targets = [r1, r2, r3]
    copies = [[None] * windows for _ in range(3)]

    def send(stage, w):
        keep = keep_bit(stage, w)
        source = x_ref.at[w, 1 - keep] if stage == 0 else outgoing[stage].at[w]
        copy = pltpu.make_async_remote_copy(
            src_ref=source,
            dst_ref=targets[stage].at[w],
            send_sem=sends.at[stage, w],
            recv_sem=recvs.at[stage, w],
            device_id=(dcn, blk, partners[stage]),
            device_id_type=mesh_id,
        )
        copy.start()
        copies[stage][w] = copy

    def back_copy(w, half, slot, target):
        return pltpu.make_async_remote_copy(
            src_ref=a3.at[w, half],
            dst_ref=back.at[w, slot],
            send_sem=sends.at[3 + half, w],
            recv_sem=recvs.at[3 + slot, w],
            device_id=target,
            device_id_type=mesh_id,
        )

    def outgoing_back(w, half):
        return back_copy(w, half, bits[2], device(block - (WIN - w), owner(w, half)))

    for w in range(windows):
        send(0, w)
    for stage in range(2):
        for w in range(windows):
            copies[stage][w].wait_recv()
            arrived = targets[stage][w].astype(jnp.float32)
            summed = kept[stage][w, keep_bit(stage, w)].astype(jnp.float32) + arrived
            kept[stage + 1][w] = summed
            if stage == 1 and w < WIN:
                a3[w] = summed.astype(a3.dtype)
                for half in range(2):

                    @pl.when(sends_back[w])
                    def _():
                        outgoing_back(w, half).start()

            else:
                away = kept[stage + 1][w, 1 - keep_bit(stage + 1, w)]
                outgoing[stage + 1][w] = away.astype(outgoing[stage + 1].dtype)
                send(stage + 1, w)
    copies[2][WIN].wait_recv()
    total[...] = a2[WIN, bits[2]] + r3[WIN].astype(jnp.float32)
    for w in range(WIN - 1, -1, -1):
        for slot in range(2):

            @pl.when(gets_back[w])
            def _():
                back_copy(w, 0, slot, device(block + WIN - w, sender(w, slot))).wait_recv()
                total[...] = total[...] + back[w, slot].astype(jnp.float32)

    o_ref[...] = total[...]
    for stage in range(3):
        for w in range(windows):
            if copies[stage][w] is not None:
                copies[stage][w].wait_send()
    for w in range(WIN):
        for half in range(2):

            @pl.when(sends_back[w])
            def _():
                outgoing_back(w, half).wait_send()


def grad_reduce(chunks, width, dtype):
    windows, rest = chunks.shape[0], chunks.shape[4:]
    f32 = jnp.float32
    link = jnp.bfloat16
    total = pl.pallas_call(
        grad_reduce_kernel,
        out_shape=jax.ShapeDtypeStruct(rest, f32),
        in_specs=[pl.BlockSpec(memory_space=pltpu.VMEM)],
        out_specs=pl.BlockSpec(memory_space=pltpu.VMEM),
        scratch_shapes=[
            pltpu.VMEM((windows, 2, 2) + rest, link),
            pltpu.VMEM((windows, 2) + rest, link),
            pltpu.VMEM((windows,) + rest, link),
            pltpu.VMEM((windows, 2, 2) + rest, f32),
            pltpu.VMEM((windows, 2) + rest, f32),
            pltpu.VMEM((windows, 2) + rest, link),
            pltpu.VMEM((windows,) + rest, link),
            pltpu.VMEM((WIN, 2) + rest, link),
            pltpu.VMEM(rest, f32),
            pltpu.VMEM((WIN, 2) + rest, link),
            pltpu.SemaphoreType.DMA((5, windows)),
            pltpu.SemaphoreType.DMA((5, windows)),
        ],
        compiler_params=pltpu.CompilerParams(collective_id=0, has_side_effects=True),
    )(chunks)
    return total[:, :width].astype(dtype), total[:, width:].astype(dtype)


def attention_kernel(q_ref, d_ref, w_ref, s_ref, dq_ref, t_ref, dk_acc, dv_acc):
    heads, rows, width = q_ref.shape
    span = w_ref.shape[1]
    tile = 128
    reach = min(span, WIN * rows + tile)
    scale = width ** (-0.5)
    f32 = jnp.float32
    dk_acc[...] = jnp.zeros_like(dk_acc)
    dv_acc[...] = jnp.zeros_like(dv_acc)
    contract_last = (((1,), (1,)), ((), ()))
    contract_first = (((0,), (0,)), ((), ()))
    for h in range(heads):
        for r0 in range(0, rows, tile):
            k0 = min(r0, span - reach)
            qt = q_ref[h, r0 : r0 + tile, :]
            dt = d_ref[h, r0 : r0 + tile, :]
            kt = w_ref[0, k0 : k0 + reach, :]
            vt = w_ref[1, k0 : k0 + reach, :]
            starts = s_ref[r0 : r0 + tile, :]
            row = r0 + lax.broadcasted_iota(jnp.int32, (tile, reach), 0)
            col = k0 + lax.broadcasted_iota(jnp.int32, (tile, reach), 1)
            visible = (col >= starts) & (col <= row + WIN * rows)
            scores = lax.dot_general(qt, kt, contract_last, preferred_element_type=f32) * scale
            top = jnp.max(jnp.where(visible, scores, -1e30), axis=1, keepdims=True)
            expo = jnp.where(visible, jnp.exp(scores - top), 0.0)
            prob = expo / jnp.sum(expo, axis=1, keepdims=True)
            prob_low = prob.astype(jnp.bfloat16)
            attended = jnp.dot(prob_low, vt, preferred_element_type=f32)
            delta = jnp.sum(dt.astype(f32) * attended, axis=1, keepdims=True)
            dprob = lax.dot_general(dt, vt, contract_last, preferred_element_type=f32)
            dscore = (prob * (dprob - delta)).astype(jnp.bfloat16)
            dq = jnp.dot(dscore, kt, preferred_element_type=f32) * scale
            dq_ref[h, r0 : r0 + tile, :] = dq.astype(dq_ref.dtype)
            dk_acc[k0 : k0 + reach, :] += lax.dot_general(dscore, qt, contract_first, preferred_element_type=f32)
            dv_acc[k0 : k0 + reach, :] += lax.dot_general(prob_low, dt, contract_first, preferred_element_type=f32)
    piece = t_ref.shape[4]
    for w in range(t_ref.shape[0]):
        for c in range(rows // piece):
            first = w * rows + c * piece
            place = (w, c % 2, (c // 2) % 2, c // 4)
            dk = dk_acc[first : first + piece, :] * scale
            t_ref[place + (slice(None), slice(0, width))] = dk.astype(t_ref.dtype)
            t_ref[place + (slice(None), slice(width, 2 * width))] = dv_acc[first : first + piece, :].astype(t_ref.dtype)


def attention(q, dout, window, starts, parts):
    heads, rows, width = q.shape
    span = window.shape[1]
    f32 = jnp.float32
    piece = rows // parts
    vmem = pl.BlockSpec(memory_space=pltpu.VMEM)
    return pl.pallas_call(
        attention_kernel,
        out_shape=(
            jax.ShapeDtypeStruct(q.shape, q.dtype),
            jax.ShapeDtypeStruct((span // rows, 2, 2, 2, piece, 2 * width), jnp.bfloat16),
        ),
        in_specs=[vmem] * 4,
        out_specs=(vmem, vmem),
        scratch_shapes=[pltpu.VMEM((span, width), f32), pltpu.VMEM((span, width), f32)],
    )(q, dout, window, starts)


def local_grads(q, dout, starts, kwin, value_window, qpos, kpos):
    scale = q.shape[-1] ** (-0.5)
    visible = (kpos[None, :] >= starts[:, None]) & (kpos[None, :] <= qpos[:, None])
    scores = jnp.einsum("ihe,je->hij", q, kwin, preferred_element_type=jnp.float32) * scale
    top = jnp.max(jnp.where(visible[None], scores, -1e30), axis=-1, keepdims=True)
    expo = jnp.where(visible[None], jnp.exp(scores - top), 0.0)
    lse = top + jnp.log(jnp.sum(expo, axis=-1, keepdims=True))
    prob = jnp.where(visible[None], jnp.exp(scores - lse), 0.0)
    prob_low = prob.astype(jnp.bfloat16)
    attended_keys = jnp.einsum(
        "hij,je->ihe", prob_low, value_window, preferred_element_type=jnp.float32
    )
    delta = jnp.sum(dout.astype(jnp.float32) * attended_keys, axis=-1)
    dprob = jnp.einsum("ihe,je->hij", dout, value_window, preferred_element_type=jnp.float32)
    dscore = (prob * (dprob - jnp.transpose(delta)[:, :, None])).astype(jnp.bfloat16)
    dq = (
        jnp.einsum("hij,je->ihe", dscore, kwin, preferred_element_type=jnp.float32) * scale
    ).astype(jnp.bfloat16)
    dk = jnp.einsum("hij,ihe->je", dscore, q, preferred_element_type=jnp.float32) * scale
    dv = jnp.einsum("hij,ihe->je", prob_low, dout, preferred_element_type=jnp.float32)
    return (dq, jnp.concatenate([dk, dv], axis=1))


def body(queries, keys, values, out_grad, doc_start):
    rows = keys.shape[0]
    window_width = keys.shape[1]
    local_heads = queries.shape[1]
    position = lax.axis_index(("dcn", "blk"))
    packed = jnp.stack([keys, values])
    pieces = []
    for step in range(WIN, 0, -1):
        if step == 1:
            pieces.append(nearest_next(packed))
        else:
            pieces.append(from_behind(packed, ("dcn", "blk"), step))
    pieces.append(packed)
    window = jnp.concatenate(pieces, axis=1)
    window_span = (WIN + 1) * rows
    first_position = position * rows
    qpos = first_position + jnp.arange(rows, dtype=jnp.int32)
    kpos = first_position - WIN * rows + jnp.arange(window_span, dtype=jnp.int32)
    parts = lax.axis_size("head")
    window_start = first_position - WIN * rows
    starts = (doc_start - window_start).reshape(rows, 1)
    dq, chunks = attention(
        jnp.transpose(queries, (1, 0, 2)),
        jnp.transpose(out_grad, (1, 0, 2)),
        window,
        starts,
        parts,
    )
    q_grad = jnp.transpose(dq, (1, 0, 2))
    k_grad, v_grad = grad_reduce(chunks, window_width, jnp.bfloat16)
    return (q_grad, k_grad, v_grad)


def solution(mesh):
    in_specs = (
        P(("dcn", "blk"), "head", None),
        P(("dcn", "blk"), None),
        P(("dcn", "blk"), None),
        P(("dcn", "blk"), "head", None),
        P(("dcn", "blk")),
    )
    out_specs = (
        P(("dcn", "blk"), "head", None),
        P(("dcn", "blk", "head"), None),
        P(("dcn", "blk", "head"), None),
    )
    return jax.shard_map(body, mesh=mesh, in_specs=in_specs, out_specs=out_specs, check_vma=False)
```

```python
import jax
import jax.numpy as jnp
from jax import lax
from jax.sharding import PartitionSpec as P
from jax.experimental import pallas as pl
from jax.experimental.pallas import tpu as pltpu

WIN = 2


def from_behind(block, axis, distance):
    devices = range(lax.axis_size(axis))
    route = [(i - distance, i) for i in devices if i - distance in devices]
    return lax.ppermute(block, axis, route)


def mirror(head, parts):
    lanes = parts // 2
    return (lanes - 1 - head // 2) * 2 + head % 2


def nearest_next(block, back=False):
    parts = lax.axis_size("head")
    blocks = lax.axis_size(("dcn", "blk"))
    route = []
    for b in range(blocks - 1):
        for h in range(parts):
            pair = (b * parts + h, (b + 1) * parts + mirror(h, parts))
            route.append(pair[::-1] if back else pair)
    return lax.ppermute(block, ("dcn", "blk", "head"), route)


def grad_reduce_kernel(x_ref, o_ref, r1, r2, r3, a1, a2, t1, t2, a3, total, back, sends, recvs):
    mesh_id = pl.DeviceIdType.MESH
    dcn = lax.axis_index("dcn")
    blk = lax.axis_index("blk")
    head = lax.axis_index("head")
    per_dcn = lax.axis_size("blk")
    blocks = lax.axis_size("dcn") * per_dcn
    block = dcn * per_dcn + blk
    bits = [head % 2, (head // 2) % 2, (head // 4) % 2]
    partners = [head + 1 - 2 * bits[0], head + 2 - 4 * bits[1], head + 4 - 8 * bits[2]]

    def device(b, h):
        return (b // per_dcn, b % per_dcn, h)

    def keep_bit(stage, w):
        if stage > 0 and w == WIN - 1:
            return 1 - bits[stage]
        return bits[stage]

    def owner(w, half):
        return bits[0] + 2 * keep_bit(1, w) + 4 * half

    def sender(w, slot):
        second = bits[1] if w != WIN - 1 else 1 - bits[1]
        return bits[0] + 2 * second + 4 * slot

    sends_back = [block >= WIN - w for w in range(WIN)]
    gets_back = [block + WIN - w < blocks for w in range(WIN)]
    barrier = pltpu.get_barrier_semaphore()
    for partner in partners:
        pl.semaphore_signal(barrier, 1, device_id=(dcn, blk, partner), device_id_type=mesh_id)
    peers = len(partners)
    for w in range(WIN):
        distance = WIN - w
        for half in range(2):

            @pl.when(sends_back[w])
            def _():
                pl.semaphore_signal(barrier, 1, device_id=device(block - distance, owner(w, half)), device_id_type=mesh_id)

            @pl.when(gets_back[w])
            def _():
                pl.semaphore_signal(barrier, 1, device_id=device(block + distance, sender(w, half)), device_id_type=mesh_id)

        peers = peers + 2 * sends_back[w].astype(jnp.int32) + 2 * gets_back[w].astype(jnp.int32)
    pl.semaphore_wait(barrier, peers)

    windows = x_ref.shape[0]
    kept = [x_ref, a1, a2]
    outgoing = [None, t1, t2]
    targets = [r1, r2, r3]
    copies = [[None] * windows for _ in range(3)]

    def send(stage, w):
        keep = keep_bit(stage, w)
        source = x_ref.at[w, 1 - keep] if stage == 0 else outgoing[stage].at[w]
        copy = pltpu.make_async_remote_copy(
            src_ref=source,
            dst_ref=targets[stage].at[w],
            send_sem=sends.at[stage, w],
            recv_sem=recvs.at[stage, w],
            device_id=(dcn, blk, partners[stage]),
            device_id_type=mesh_id,
        )
        copy.start()
        copies[stage][w] = copy

    def back_copy(w, half, slot, target):
        return pltpu.make_async_remote_copy(
            src_ref=a3.at[w, half],
            dst_ref=back.at[w, slot],
            send_sem=sends.at[3 + half, w],
            recv_sem=recvs.at[3 + slot, w],
            device_id=target,
            device_id_type=mesh_id,
        )

    def outgoing_back(w, half):
        return back_copy(w, half, bits[2], device(block - (WIN - w), owner(w, half)))

    for w in range(windows):
        send(0, w)
    for stage in range(2):
        for w in range(windows):
            copies[stage][w].wait_recv()
            arrived = targets[stage][w].astype(jnp.float32)
            summed = kept[stage][w, keep_bit(stage, w)].astype(jnp.float32) + arrived
            kept[stage + 1][w] = summed
            if stage == 1 and w < WIN:
                a3[w] = summed.astype(a3.dtype)
                for half in range(2):

                    @pl.when(sends_back[w])
                    def _():
                        outgoing_back(w, half).start()

            else:
                away = kept[stage + 1][w, 1 - keep_bit(stage + 1, w)]
                outgoing[stage + 1][w] = away.astype(outgoing[stage + 1].dtype)
                send(stage + 1, w)
    copies[2][WIN].wait_recv()
    total[...] = a2[WIN, bits[2]] + r3[WIN].astype(jnp.float32)
    for w in range(WIN - 1, -1, -1):
        for slot in range(2):

            @pl.when(gets_back[w])
            def _():
                back_copy(w, 0, slot, device(block + WIN - w, sender(w, slot))).wait_recv()
                total[...] = total[...] + back[w, slot].astype(jnp.float32)

    o_ref[...] = total[...]
    for stage in range(3):
        for w in range(windows):
            if copies[stage][w] is not None:
                copies[stage][w].wait_send()
    for w in range(WIN):
        for half in range(2):

            @pl.when(sends_back[w])
            def _():
                outgoing_back(w, half).wait_send()


def grad_reduce(chunks, width, dtype):
    windows, rest = chunks.shape[0], chunks.shape[4:]
    f32 = jnp.float32
    link = jnp.bfloat16
    total = pl.pallas_call(
        grad_reduce_kernel,
        out_shape=jax.ShapeDtypeStruct(rest, f32),
        in_specs=[pl.BlockSpec(memory_space=pltpu.VMEM)],
        out_specs=pl.BlockSpec(memory_space=pltpu.VMEM),
        scratch_shapes=[
            pltpu.VMEM((windows, 2, 2) + rest, link),
            pltpu.VMEM((windows, 2) + rest, link),
            pltpu.VMEM((windows,) + rest, link),
            pltpu.VMEM((windows, 2, 2) + rest, f32),
            pltpu.VMEM((windows, 2) + rest, f32),
            pltpu.VMEM((windows, 2) + rest, link),
            pltpu.VMEM((windows,) + rest, link),
            pltpu.VMEM((WIN, 2) + rest, link),
            pltpu.VMEM(rest, f32),
            pltpu.VMEM((WIN, 2) + rest, link),
            pltpu.SemaphoreType.DMA((5, windows)),
            pltpu.SemaphoreType.DMA((5, windows)),
        ],
        compiler_params=pltpu.CompilerParams(collective_id=0, has_side_effects=True),
    )(chunks)
    return total[:, :width].astype(dtype), total[:, width:].astype(dtype)


def attention_kernel(q_ref, d_ref, w_ref, s_ref, dq_ref, t_ref, dk_acc, dv_acc):
    rows, width = q_ref.shape[0], w_ref.shape[2]
    heads = q_ref.shape[1] // width
    span = w_ref.shape[1]
    tile = 128
    reach = min(span, WIN * rows + tile)
    scale = width ** (-0.5)
    f32 = jnp.float32
    dk_acc[...] = jnp.zeros_like(dk_acc)
    dv_acc[...] = jnp.zeros_like(dv_acc)
    contract_last = (((1,), (1,)), ((), ()))
    contract_first = (((0,), (0,)), ((), ()))
    for h in range(heads):
        for r0 in range(0, rows, tile):
            k0 = min(r0, span - reach)
            lanes = slice(h * width, (h + 1) * width)
            qt = q_ref[r0 : r0 + tile, lanes]
            dt = d_ref[r0 : r0 + tile, lanes]
            kt = w_ref[0, k0 : k0 + reach, :]
            vt = w_ref[1, k0 : k0 + reach, :]
            starts = s_ref[r0 : r0 + tile, :]
            row = r0 + lax.broadcasted_iota(jnp.int32, (tile, reach), 0)
            col = k0 + lax.broadcasted_iota(jnp.int32, (tile, reach), 1)
            visible = (col >= starts) & (col <= row + WIN * rows)
            scores = lax.dot_general(qt, kt, contract_last, preferred_element_type=f32) * scale
            top = jnp.max(jnp.where(visible, scores, -1e30), axis=1, keepdims=True)
            expo = jnp.where(visible, jnp.exp(scores - top), 0.0)
            prob = expo / jnp.sum(expo, axis=1, keepdims=True)
            prob_low = prob.astype(jnp.bfloat16)
            attended = jnp.dot(prob_low, vt, preferred_element_type=f32)
            delta = jnp.sum(dt.astype(f32) * attended, axis=1, keepdims=True)
            dprob = lax.dot_general(dt, vt, contract_last, preferred_element_type=f32)
            dscore = (prob * (dprob - delta)).astype(jnp.bfloat16)
            dq = jnp.dot(dscore, kt, preferred_element_type=f32) * scale
            dq_ref[r0 : r0 + tile, lanes] = dq.astype(dq_ref.dtype)
            dk_acc[k0 : k0 + reach, :] += lax.dot_general(dscore, qt, contract_first, preferred_element_type=f32)
            dv_acc[k0 : k0 + reach, :] += lax.dot_general(prob_low, dt, contract_first, preferred_element_type=f32)
    piece = t_ref.shape[4]
    for w in range(t_ref.shape[0]):
        for c in range(rows // piece):
            first = w * rows + c * piece
            place = (w, c % 2, (c // 2) % 2, c // 4)
            dk = dk_acc[first : first + piece, :] * scale
            t_ref[place + (slice(None), slice(0, width))] = dk.astype(t_ref.dtype)
            t_ref[place + (slice(None), slice(width, 2 * width))] = dv_acc[first : first + piece, :].astype(t_ref.dtype)


def attention(q, dout, window, starts, parts):
    rows, width = q.shape[0], window.shape[2]
    span = window.shape[1]
    f32 = jnp.float32
    piece = rows // parts
    vmem = pl.BlockSpec(memory_space=pltpu.VMEM)
    return pl.pallas_call(
        attention_kernel,
        out_shape=(
            jax.ShapeDtypeStruct(q.shape, q.dtype),
            jax.ShapeDtypeStruct((span // rows, 2, 2, 2, piece, 2 * width), jnp.bfloat16),
        ),
        in_specs=[vmem] * 4,
        out_specs=(vmem, vmem),
        scratch_shapes=[pltpu.VMEM((span, width), f32), pltpu.VMEM((span, width), f32)],
    )(q, dout, window, starts)


def local_grads(q, dout, starts, kwin, value_window, qpos, kpos):
    scale = q.shape[-1] ** (-0.5)
    visible = (kpos[None, :] >= starts[:, None]) & (kpos[None, :] <= qpos[:, None])
    scores = jnp.einsum("ihe,je->hij", q, kwin, preferred_element_type=jnp.float32) * scale
    top = jnp.max(jnp.where(visible[None], scores, -1e30), axis=-1, keepdims=True)
    expo = jnp.where(visible[None], jnp.exp(scores - top), 0.0)
    lse = top + jnp.log(jnp.sum(expo, axis=-1, keepdims=True))
    prob = jnp.where(visible[None], jnp.exp(scores - lse), 0.0)
    prob_low = prob.astype(jnp.bfloat16)
    attended_keys = jnp.einsum(
        "hij,je->ihe", prob_low, value_window, preferred_element_type=jnp.float32
    )
    delta = jnp.sum(dout.astype(jnp.float32) * attended_keys, axis=-1)
    dprob = jnp.einsum("ihe,je->hij", dout, value_window, preferred_element_type=jnp.float32)
    dscore = (prob * (dprob - jnp.transpose(delta)[:, :, None])).astype(jnp.bfloat16)
    dq = (
        jnp.einsum("hij,je->ihe", dscore, kwin, preferred_element_type=jnp.float32) * scale
    ).astype(jnp.bfloat16)
    dk = jnp.einsum("hij,ihe->je", dscore, q, preferred_element_type=jnp.float32) * scale
    dv = jnp.einsum("hij,ihe->je", prob_low, dout, preferred_element_type=jnp.float32)
    return (dq, jnp.concatenate([dk, dv], axis=1))


def body(queries, keys, values, out_grad, doc_start):
    rows = keys.shape[0]
    window_width = keys.shape[1]
    local_heads = queries.shape[1]
    position = lax.axis_index(("dcn", "blk"))
    packed = jnp.stack([keys, values])
    pieces = []
    for step in range(WIN, 0, -1):
        if step == 1:
            pieces.append(nearest_next(packed))
        else:
            pieces.append(from_behind(packed, ("dcn", "blk"), step))
    pieces.append(packed)
    window = jnp.concatenate(pieces, axis=1)
    window_span = (WIN + 1) * rows
    first_position = position * rows
    qpos = first_position + jnp.arange(rows, dtype=jnp.int32)
    kpos = first_position - WIN * rows + jnp.arange(window_span, dtype=jnp.int32)
    parts = lax.axis_size("head")
    window_start = first_position - WIN * rows
    starts = (doc_start - window_start).reshape(rows, 1)
    dq, chunks = attention(
        queries.reshape(rows, -1),
        out_grad.reshape(rows, -1),
        window,
        starts,
        parts,
    )
    q_grad = dq.reshape(queries.shape)
    k_grad, v_grad = grad_reduce(chunks, window_width, jnp.bfloat16)
    return (q_grad, k_grad, v_grad)


def solution(mesh):
    in_specs = (
        P(("dcn", "blk"), "head", None),
        P(("dcn", "blk"), None),
        P(("dcn", "blk"), None),
        P(("dcn", "blk"), "head", None),
        P(("dcn", "blk")),
    )
    out_specs = (
        P(("dcn", "blk"), "head", None),
        P(("dcn", "blk", "head"), None),
        P(("dcn", "blk", "head"), None),
    )
    return jax.shard_map(body, mesh=mesh, in_specs=in_specs, out_specs=out_specs, check_vma=False)
```

```python
import jax
import jax.numpy as jnp
from jax import lax
from jax.sharding import PartitionSpec as P
from jax.experimental import pallas as pl
from jax.experimental.pallas import tpu as pltpu

WIN = 2


def from_behind(block, axis, distance):
    devices = range(lax.axis_size(axis))
    route = [(i - distance, i) for i in devices if i - distance in devices]
    return lax.ppermute(block, axis, route)


def mirror(head, parts):
    lanes = parts // 2
    return (lanes - 1 - head // 2) * 2 + head % 2


def nearest_next(block, back=False):
    parts = lax.axis_size("head")
    blocks = lax.axis_size(("dcn", "blk"))
    route = []
    for b in range(blocks - 1):
        for h in range(parts):
            pair = (b * parts + h, (b + 1) * parts + mirror(h, parts))
            route.append(pair[::-1] if back else pair)
    return lax.ppermute(block, ("dcn", "blk", "head"), route)


def grad_reduce_kernel(x_ref, o_ref, r1, r2, r3, a1, a2, t1, t2, a3, total, back, sends, recvs):
    mesh_id = pl.DeviceIdType.MESH
    dcn = lax.axis_index("dcn")
    blk = lax.axis_index("blk")
    head = lax.axis_index("head")
    per_dcn = lax.axis_size("blk")
    blocks = lax.axis_size("dcn") * per_dcn
    block = dcn * per_dcn + blk
    bits = [head % 2, (head // 2) % 2, (head // 4) % 2]
    partners = [head + 1 - 2 * bits[0], head + 2 - 4 * bits[1], head + 4 - 8 * bits[2]]

    def device(b, h):
        return (b // per_dcn, b % per_dcn, h)

    def keep_bit(stage, w):
        if stage > 0 and w == WIN - 1:
            return 1 - bits[stage]
        return bits[stage]

    def owner(w, half):
        return bits[0] + 2 * keep_bit(1, w) + 4 * half

    def sender(w, slot):
        second = bits[1] if w != WIN - 1 else 1 - bits[1]
        return bits[0] + 2 * second + 4 * slot

    sends_back = [block >= WIN - w for w in range(WIN)]
    gets_back = [block + WIN - w < blocks for w in range(WIN)]
    barrier = pltpu.get_barrier_semaphore()
    for partner in partners:
        pl.semaphore_signal(barrier, 1, device_id=(dcn, blk, partner), device_id_type=mesh_id)
    peers = len(partners)
    for w in range(WIN):
        distance = WIN - w
        for half in range(2):

            @pl.when(sends_back[w])
            def _():
                pl.semaphore_signal(barrier, 1, device_id=device(block - distance, owner(w, half)), device_id_type=mesh_id)

            @pl.when(gets_back[w])
            def _():
                pl.semaphore_signal(barrier, 1, device_id=device(block + distance, sender(w, half)), device_id_type=mesh_id)

        peers = peers + 2 * sends_back[w].astype(jnp.int32) + 2 * gets_back[w].astype(jnp.int32)
    pl.semaphore_wait(barrier, peers)

    windows = x_ref.shape[0]
    kept = [x_ref, a1, a2]
    outgoing = [None, t1, t2]
    targets = [r1, r2, r3]
    copies = [[None] * windows for _ in range(3)]

    def send(stage, w):
        keep = keep_bit(stage, w)
        source = x_ref.at[w, 1 - keep] if stage == 0 else outgoing[stage].at[w]
        copy = pltpu.make_async_remote_copy(
            src_ref=source,
            dst_ref=targets[stage].at[w],
            send_sem=sends.at[stage, w],
            recv_sem=recvs.at[stage, w],
            device_id=(dcn, blk, partners[stage]),
            device_id_type=mesh_id,
        )
        copy.start()
        copies[stage][w] = copy

    def back_copy(w, half, slot, target):
        return pltpu.make_async_remote_copy(
            src_ref=a3.at[w, half],
            dst_ref=back.at[w, slot],
            send_sem=sends.at[3 + half, w],
            recv_sem=recvs.at[3 + slot, w],
            device_id=target,
            device_id_type=mesh_id,
        )

    def outgoing_back(w, half):
        return back_copy(w, half, bits[2], device(block - (WIN - w), owner(w, half)))

    for w in range(windows):
        send(0, w)
    for stage in range(2):
        for w in range(windows):
            copies[stage][w].wait_recv()
            arrived = targets[stage][w].astype(jnp.float32)
            summed = kept[stage][w, keep_bit(stage, w)].astype(jnp.float32) + arrived
            kept[stage + 1][w] = summed
            if stage == 1 and w < WIN:
                a3[w] = summed.astype(a3.dtype)
                for half in range(2):

                    @pl.when(sends_back[w])
                    def _():
                        outgoing_back(w, half).start()

            else:
                away = kept[stage + 1][w, 1 - keep_bit(stage + 1, w)]
                outgoing[stage + 1][w] = away.astype(outgoing[stage + 1].dtype)
                send(stage + 1, w)
    copies[2][WIN].wait_recv()
    total[...] = a2[WIN, bits[2]] + r3[WIN].astype(jnp.float32)
    for w in range(WIN - 1, -1, -1):
        for slot in range(2):

            @pl.when(gets_back[w])
            def _():
                back_copy(w, 0, slot, device(block + WIN - w, sender(w, slot))).wait_recv()
                total[...] = total[...] + back[w, slot].astype(jnp.float32)

    o_ref[...] = total[...].astype(o_ref.dtype)
    for stage in range(3):
        for w in range(windows):
            if copies[stage][w] is not None:
                copies[stage][w].wait_send()
    for w in range(WIN):
        for half in range(2):

            @pl.when(sends_back[w])
            def _():
                outgoing_back(w, half).wait_send()


def grad_reduce(chunks, width, dtype):
    windows, rest = chunks.shape[0], chunks.shape[4:]
    f32 = jnp.float32
    link = jnp.bfloat16
    total = pl.pallas_call(
        grad_reduce_kernel,
        out_shape=jax.ShapeDtypeStruct(rest, dtype),
        in_specs=[pl.BlockSpec(memory_space=pltpu.VMEM)],
        out_specs=pl.BlockSpec(memory_space=pltpu.VMEM),
        scratch_shapes=[
            pltpu.VMEM((windows, 2, 2) + rest, link),
            pltpu.VMEM((windows, 2) + rest, link),
            pltpu.VMEM((windows,) + rest, link),
            pltpu.VMEM((windows, 2, 2) + rest, f32),
            pltpu.VMEM((windows, 2) + rest, f32),
            pltpu.VMEM((windows, 2) + rest, link),
            pltpu.VMEM((windows,) + rest, link),
            pltpu.VMEM((WIN, 2) + rest, link),
            pltpu.VMEM(rest, f32),
            pltpu.VMEM((WIN, 2) + rest, link),
            pltpu.SemaphoreType.DMA((5, windows)),
            pltpu.SemaphoreType.DMA((5, windows)),
        ],
        compiler_params=pltpu.CompilerParams(collective_id=0, has_side_effects=True),
    )(chunks)
    return total[:, :width], total[:, width:]


def attention_kernel(q_ref, d_ref, w_ref, s_ref, dq_ref, t_ref, dk_acc, dv_acc):
    rows, width = q_ref.shape[0], w_ref.shape[2]
    heads = q_ref.shape[1] // width
    span = w_ref.shape[1]
    tile = 128
    reach = min(span, WIN * rows + tile)
    scale = width ** (-0.5)
    f32 = jnp.float32
    dk_acc[...] = jnp.zeros_like(dk_acc)
    dv_acc[...] = jnp.zeros_like(dv_acc)
    contract_last = (((1,), (1,)), ((), ()))
    contract_first = (((0,), (0,)), ((), ()))
    for h in range(heads):
        for r0 in range(0, rows, tile):
            k0 = min(r0, span - reach)
            lanes = slice(h * width, (h + 1) * width)
            qt = q_ref[r0 : r0 + tile, lanes]
            dt = d_ref[r0 : r0 + tile, lanes]
            kt = w_ref[0, k0 : k0 + reach, :]
            vt = w_ref[1, k0 : k0 + reach, :]
            starts = s_ref[r0 : r0 + tile, :]
            row = r0 + lax.broadcasted_iota(jnp.int32, (tile, reach), 0)
            col = k0 + lax.broadcasted_iota(jnp.int32, (tile, reach), 1)
            visible = (col >= starts) & (col <= row + WIN * rows)
            scores = lax.dot_general(qt, kt, contract_last, preferred_element_type=f32) * scale
            top = jnp.max(jnp.where(visible, scores, -1e30), axis=1, keepdims=True)
            expo = jnp.where(visible, jnp.exp(scores - top), 0.0)
            prob = expo / jnp.sum(expo, axis=1, keepdims=True)
            prob_low = prob.astype(jnp.bfloat16)
            attended = jnp.dot(prob_low, vt, preferred_element_type=f32)
            delta = jnp.sum(dt.astype(f32) * attended, axis=1, keepdims=True)
            dprob = lax.dot_general(dt, vt, contract_last, preferred_element_type=f32)
            dscore = (prob * (dprob - delta)).astype(jnp.bfloat16)
            dq = jnp.dot(dscore, kt, preferred_element_type=f32) * scale
            dq_ref[r0 : r0 + tile, lanes] = dq.astype(dq_ref.dtype)
            dk_acc[k0 : k0 + reach, :] += lax.dot_general(dscore, qt, contract_first, preferred_element_type=f32)
            dv_acc[k0 : k0 + reach, :] += lax.dot_general(prob_low, dt, contract_first, preferred_element_type=f32)
    piece = t_ref.shape[4]
    for w in range(t_ref.shape[0]):
        for c in range(rows // piece):
            first = w * rows + c * piece
            place = (w, c % 2, (c // 2) % 2, c // 4)
            dk = dk_acc[first : first + piece, :] * scale
            t_ref[place + (slice(None), slice(0, width))] = dk.astype(t_ref.dtype)
            t_ref[place + (slice(None), slice(width, 2 * width))] = dv_acc[first : first + piece, :].astype(t_ref.dtype)


def attention(q, dout, window, starts, parts):
    rows, width = q.shape[0], window.shape[2]
    span = window.shape[1]
    f32 = jnp.float32
    piece = rows // parts
    vmem = pl.BlockSpec(memory_space=pltpu.VMEM)
    return pl.pallas_call(
        attention_kernel,
        out_shape=(
            jax.ShapeDtypeStruct(q.shape, q.dtype),
            jax.ShapeDtypeStruct((span // rows, 2, 2, 2, piece, 2 * width), jnp.bfloat16),
        ),
        in_specs=[vmem] * 4,
        out_specs=(vmem, vmem),
        scratch_shapes=[pltpu.VMEM((span, width), f32), pltpu.VMEM((span, width), f32)],
    )(q, dout, window, starts)


def local_grads(q, dout, starts, kwin, value_window, qpos, kpos):
    scale = q.shape[-1] ** (-0.5)
    visible = (kpos[None, :] >= starts[:, None]) & (kpos[None, :] <= qpos[:, None])
    scores = jnp.einsum("ihe,je->hij", q, kwin, preferred_element_type=jnp.float32) * scale
    top = jnp.max(jnp.where(visible[None], scores, -1e30), axis=-1, keepdims=True)
    expo = jnp.where(visible[None], jnp.exp(scores - top), 0.0)
    lse = top + jnp.log(jnp.sum(expo, axis=-1, keepdims=True))
    prob = jnp.where(visible[None], jnp.exp(scores - lse), 0.0)
    prob_low = prob.astype(jnp.bfloat16)
    attended_keys = jnp.einsum(
        "hij,je->ihe", prob_low, value_window, preferred_element_type=jnp.float32
    )
    delta = jnp.sum(dout.astype(jnp.float32) * attended_keys, axis=-1)
    dprob = jnp.einsum("ihe,je->hij", dout, value_window, preferred_element_type=jnp.float32)
    dscore = (prob * (dprob - jnp.transpose(delta)[:, :, None])).astype(jnp.bfloat16)
    dq = (
        jnp.einsum("hij,je->ihe", dscore, kwin, preferred_element_type=jnp.float32) * scale
    ).astype(jnp.bfloat16)
    dk = jnp.einsum("hij,ihe->je", dscore, q, preferred_element_type=jnp.float32) * scale
    dv = jnp.einsum("hij,ihe->je", prob_low, dout, preferred_element_type=jnp.float32)
    return (dq, jnp.concatenate([dk, dv], axis=1))


def body(queries, keys, values, out_grad, doc_start):
    rows = keys.shape[0]
    window_width = keys.shape[1]
    local_heads = queries.shape[1]
    position = lax.axis_index(("dcn", "blk"))
    packed = jnp.stack([keys, values])
    pieces = []
    for step in range(WIN, 0, -1):
        if step == 1:
            pieces.append(nearest_next(packed))
        else:
            pieces.append(from_behind(packed, ("dcn", "blk"), step))
    pieces.append(packed)
    window = jnp.concatenate(pieces, axis=1)
    window_span = (WIN + 1) * rows
    first_position = position * rows
    qpos = first_position + jnp.arange(rows, dtype=jnp.int32)
    kpos = first_position - WIN * rows + jnp.arange(window_span, dtype=jnp.int32)
    parts = lax.axis_size("head")
    window_start = first_position - WIN * rows
    starts = (doc_start - window_start).reshape(rows, 1)
    dq, chunks = attention(
        queries.reshape(rows, -1),
        out_grad.reshape(rows, -1),
        window,
        starts,
        parts,
    )
    q_grad = dq.reshape(queries.shape)
    k_grad, v_grad = grad_reduce(chunks, window_width, jnp.bfloat16)
    return (q_grad, k_grad, v_grad)


def solution(mesh):
    in_specs = (
        P(("dcn", "blk"), "head", None),
        P(("dcn", "blk"), None),
        P(("dcn", "blk"), None),
        P(("dcn", "blk"), "head", None),
        P(("dcn", "blk")),
    )
    out_specs = (
        P(("dcn", "blk"), "head", None),
        P(("dcn", "blk", "head"), None),
        P(("dcn", "blk", "head"), None),
    )
    return jax.shard_map(body, mesh=mesh, in_specs=in_specs, out_specs=out_specs, check_vma=False)
```

```python
import jax
import jax.numpy as jnp
from jax import lax
from jax.sharding import PartitionSpec as P
from jax.experimental import pallas as pl
from jax.experimental.pallas import tpu as pltpu

WIN = 2


def from_behind(block, axis, distance):
    devices = range(lax.axis_size(axis))
    route = [(i - distance, i) for i in devices if i - distance in devices]
    return lax.ppermute(block, axis, route)


def mirror(head, parts):
    lanes = parts // 2
    return (lanes - 1 - head // 2) * 2 + head % 2


def nearest_next(block, back=False):
    parts = lax.axis_size("head")
    blocks = lax.axis_size(("dcn", "blk"))
    route = []
    for b in range(blocks - 1):
        for h in range(parts):
            pair = (b * parts + h, (b + 1) * parts + mirror(h, parts))
            route.append(pair[::-1] if back else pair)
    return lax.ppermute(block, ("dcn", "blk", "head"), route)


def grad_reduce_kernel(x_ref, o_ref, r1, r2, r3, a1, a2, t1, t2, a3, total, back, sends, recvs):
    mesh_id = pl.DeviceIdType.MESH
    dcn = lax.axis_index("dcn")
    blk = lax.axis_index("blk")
    head = lax.axis_index("head")
    per_dcn = lax.axis_size("blk")
    blocks = lax.axis_size("dcn") * per_dcn
    block = dcn * per_dcn + blk
    bits = [head % 2, (head // 2) % 2, (head // 4) % 2]
    partners = [head + 1 - 2 * bits[0], head + 2 - 4 * bits[1], head + 4 - 8 * bits[2]]

    def device(b, h):
        return (b // per_dcn, b % per_dcn, h)

    def keep_bit(stage, w):
        if stage > 0 and w == WIN - 1:
            return 1 - bits[stage]
        return bits[stage]

    def owner(w, half):
        return bits[0] + 2 * keep_bit(1, w) + 4 * half

    def sender(w, slot):
        second = bits[1] if w != WIN - 1 else 1 - bits[1]
        return bits[0] + 2 * second + 4 * slot

    sends_back = [block >= WIN - w for w in range(WIN)]
    gets_back = [block + WIN - w < blocks for w in range(WIN)]
    barrier = pltpu.get_barrier_semaphore()
    for partner in partners:
        pl.semaphore_signal(barrier, 1, device_id=(dcn, blk, partner), device_id_type=mesh_id)
    peers = len(partners)
    for w in range(WIN):
        distance = WIN - w
        for half in range(2):

            @pl.when(sends_back[w])
            def _():
                pl.semaphore_signal(barrier, 1, device_id=device(block - distance, owner(w, half)), device_id_type=mesh_id)

            @pl.when(gets_back[w])
            def _():
                pl.semaphore_signal(barrier, 1, device_id=device(block + distance, sender(w, half)), device_id_type=mesh_id)

        peers = peers + 2 * sends_back[w].astype(jnp.int32) + 2 * gets_back[w].astype(jnp.int32)
    pl.semaphore_wait(barrier, peers)

    windows = x_ref.shape[0]
    kept = [x_ref, a1, a2]
    outgoing = [None, t1, t2]
    targets = [r1, r2, r3]
    copies = [[None] * windows for _ in range(3)]

    def send(stage, w):
        keep = keep_bit(stage, w)
        source = x_ref.at[w, 1 - keep] if stage == 0 else outgoing[stage].at[w]
        copy = pltpu.make_async_remote_copy(
            src_ref=source,
            dst_ref=targets[stage].at[w],
            send_sem=sends.at[stage, w],
            recv_sem=recvs.at[stage, w],
            device_id=(dcn, blk, partners[stage]),
            device_id_type=mesh_id,
        )
        copy.start()
        copies[stage][w] = copy

    def back_copy(w, half, slot, target):
        return pltpu.make_async_remote_copy(
            src_ref=a3.at[w, half],
            dst_ref=back.at[w, slot],
            send_sem=sends.at[3 + half, w],
            recv_sem=recvs.at[3 + slot, w],
            device_id=target,
            device_id_type=mesh_id,
        )

    def outgoing_back(w, half):
        return back_copy(w, half, bits[2], device(block - (WIN - w), owner(w, half)))

    for w in range(windows):
        send(0, w)
    for stage in range(2):
        for w in range(windows):
            copies[stage][w].wait_recv()
            arrived = targets[stage][w].astype(jnp.float32)
            summed = kept[stage][w, keep_bit(stage, w)].astype(jnp.float32) + arrived
            kept[stage + 1][w] = summed
            if stage == 1 and w < WIN:
                a3[w] = summed.astype(a3.dtype)
                for half in range(2):

                    @pl.when(sends_back[w])
                    def _():
                        outgoing_back(w, half).start()

            else:
                away = kept[stage + 1][w, 1 - keep_bit(stage + 1, w)]
                outgoing[stage + 1][w] = away.astype(outgoing[stage + 1].dtype)
                send(stage + 1, w)
    copies[2][WIN].wait_recv()
    total[...] = a2[WIN, bits[2]] + r3[WIN].astype(jnp.float32)
    for w in range(WIN - 1, -1, -1):
        for slot in range(2):

            @pl.when(gets_back[w])
            def _():
                back_copy(w, 0, slot, device(block + WIN - w, sender(w, slot))).wait_recv()
                total[...] = total[...] + back[w, slot].astype(jnp.float32)

    o_ref[...] = total[...].astype(o_ref.dtype)
    for stage in range(3):
        for w in range(windows):
            if copies[stage][w] is not None:
                copies[stage][w].wait_send()
    for w in range(WIN):
        for half in range(2):

            @pl.when(sends_back[w])
            def _():
                outgoing_back(w, half).wait_send()


def grad_reduce(chunks, width, dtype):
    windows, rest = chunks.shape[0], chunks.shape[4:]
    f32 = jnp.float32
    link = jnp.bfloat16
    total = pl.pallas_call(
        grad_reduce_kernel,
        out_shape=jax.ShapeDtypeStruct(rest, dtype),
        in_specs=[pl.BlockSpec(memory_space=pltpu.VMEM)],
        out_specs=pl.BlockSpec(memory_space=pltpu.VMEM),
        scratch_shapes=[
            pltpu.VMEM((windows, 2, 2) + rest, link),
            pltpu.VMEM((windows, 2) + rest, link),
            pltpu.VMEM((windows,) + rest, link),
            pltpu.VMEM((windows, 2, 2) + rest, f32),
            pltpu.VMEM((windows, 2) + rest, f32),
            pltpu.VMEM((windows, 2) + rest, link),
            pltpu.VMEM((windows,) + rest, link),
            pltpu.VMEM((WIN, 2) + rest, link),
            pltpu.VMEM(rest, f32),
            pltpu.VMEM((WIN, 2) + rest, link),
            pltpu.SemaphoreType.DMA((5, windows)),
            pltpu.SemaphoreType.DMA((5, windows)),
        ],
        compiler_params=pltpu.CompilerParams(collective_id=0, has_side_effects=True),
    )(chunks)
    return total[:, :width], total[:, width:]


def attention_kernel(q_ref, d_ref, far_ref, near_ref, own_ref, s_ref, dq_ref, t_ref, dk_acc, dv_acc, w_ref):
    rows, width = q_ref.shape[0], w_ref.shape[2]
    heads = q_ref.shape[1] // width
    span = w_ref.shape[1]
    tile = 128
    reach = min(span, WIN * rows + tile)
    scale = width ** (-0.5)
    f32 = jnp.float32
    for i, piece_ref in enumerate((far_ref, near_ref, own_ref)):
        w_ref[:, i * rows : (i + 1) * rows, :] = piece_ref[...]
    dk_acc[...] = jnp.zeros_like(dk_acc)
    dv_acc[...] = jnp.zeros_like(dv_acc)
    contract_last = (((1,), (1,)), ((), ()))
    contract_first = (((0,), (0,)), ((), ()))
    for h in range(heads):
        for r0 in range(0, rows, tile):
            k0 = min(r0, span - reach)
            lanes = slice(h * width, (h + 1) * width)
            qt = q_ref[r0 : r0 + tile, lanes]
            dt = d_ref[r0 : r0 + tile, lanes]
            kt = w_ref[0, k0 : k0 + reach, :]
            vt = w_ref[1, k0 : k0 + reach, :]
            starts = s_ref[r0 : r0 + tile, :]
            row = r0 + lax.broadcasted_iota(jnp.int32, (tile, reach), 0)
            col = k0 + lax.broadcasted_iota(jnp.int32, (tile, reach), 1)
            visible = (col >= starts) & (col <= row + WIN * rows)
            scores = lax.dot_general(qt, kt, contract_last, preferred_element_type=f32) * scale
            top = jnp.max(jnp.where(visible, scores, -1e30), axis=1, keepdims=True)
            expo = jnp.where(visible, jnp.exp(scores - top), 0.0)
            prob = expo / jnp.sum(expo, axis=1, keepdims=True)
            prob_low = prob.astype(jnp.bfloat16)
            attended = jnp.dot(prob_low, vt, preferred_element_type=f32)
            delta = jnp.sum(dt.astype(f32) * attended, axis=1, keepdims=True)
            dprob = lax.dot_general(dt, vt, contract_last, preferred_element_type=f32)
            dscore = (prob * (dprob - delta)).astype(jnp.bfloat16)
            dq = jnp.dot(dscore, kt, preferred_element_type=f32) * scale
            dq_ref[r0 : r0 + tile, lanes] = dq.astype(dq_ref.dtype)
            dk_acc[k0 : k0 + reach, :] += lax.dot_general(dscore, qt, contract_first, preferred_element_type=f32)
            dv_acc[k0 : k0 + reach, :] += lax.dot_general(prob_low, dt, contract_first, preferred_element_type=f32)
    piece = t_ref.shape[4]
    for w in range(t_ref.shape[0]):
        for c in range(rows // piece):
            first = w * rows + c * piece
            place = (w, c % 2, (c // 2) % 2, c // 4)
            dk = dk_acc[first : first + piece, :] * scale
            t_ref[place + (slice(None), slice(0, width))] = dk.astype(t_ref.dtype)
            t_ref[place + (slice(None), slice(width, 2 * width))] = dv_acc[first : first + piece, :].astype(t_ref.dtype)


def attention(q, dout, pieces, starts, parts):
    rows, width = q.shape[0], pieces[0].shape[2]
    span = rows * len(pieces)
    f32 = jnp.float32
    piece = rows // parts
    vmem = pl.BlockSpec(memory_space=pltpu.VMEM)
    return pl.pallas_call(
        attention_kernel,
        out_shape=(
            jax.ShapeDtypeStruct(q.shape, q.dtype),
            jax.ShapeDtypeStruct((span // rows, 2, 2, 2, piece, 2 * width), jnp.bfloat16),
        ),
        in_specs=[vmem] * 6,
        out_specs=(vmem, vmem),
        scratch_shapes=[
            pltpu.VMEM((span, width), f32),
            pltpu.VMEM((span, width), f32),
            pltpu.VMEM((2, span, width), q.dtype),
        ],
    )(q, dout, *pieces, starts)


def local_grads(q, dout, starts, kwin, value_window, qpos, kpos):
    scale = q.shape[-1] ** (-0.5)
    visible = (kpos[None, :] >= starts[:, None]) & (kpos[None, :] <= qpos[:, None])
    scores = jnp.einsum("ihe,je->hij", q, kwin, preferred_element_type=jnp.float32) * scale
    top = jnp.max(jnp.where(visible[None], scores, -1e30), axis=-1, keepdims=True)
    expo = jnp.where(visible[None], jnp.exp(scores - top), 0.0)
    lse = top + jnp.log(jnp.sum(expo, axis=-1, keepdims=True))
    prob = jnp.where(visible[None], jnp.exp(scores - lse), 0.0)
    prob_low = prob.astype(jnp.bfloat16)
    attended_keys = jnp.einsum(
        "hij,je->ihe", prob_low, value_window, preferred_element_type=jnp.float32
    )
    delta = jnp.sum(dout.astype(jnp.float32) * attended_keys, axis=-1)
    dprob = jnp.einsum("ihe,je->hij", dout, value_window, preferred_element_type=jnp.float32)
    dscore = (prob * (dprob - jnp.transpose(delta)[:, :, None])).astype(jnp.bfloat16)
    dq = (
        jnp.einsum("hij,je->ihe", dscore, kwin, preferred_element_type=jnp.float32) * scale
    ).astype(jnp.bfloat16)
    dk = jnp.einsum("hij,ihe->je", dscore, q, preferred_element_type=jnp.float32) * scale
    dv = jnp.einsum("hij,ihe->je", prob_low, dout, preferred_element_type=jnp.float32)
    return (dq, jnp.concatenate([dk, dv], axis=1))


def body(queries, keys, values, out_grad, doc_start):
    rows = keys.shape[0]
    window_width = keys.shape[1]
    local_heads = queries.shape[1]
    position = lax.axis_index(("dcn", "blk"))
    packed = jnp.stack([keys, values])
    pieces = []
    for step in range(WIN, 0, -1):
        if step == 1:
            pieces.append(nearest_next(packed))
        else:
            pieces.append(from_behind(packed, ("dcn", "blk"), step))
    pieces.append(packed)
    window_span = (WIN + 1) * rows
    first_position = position * rows
    qpos = first_position + jnp.arange(rows, dtype=jnp.int32)
    kpos = first_position - WIN * rows + jnp.arange(window_span, dtype=jnp.int32)
    parts = lax.axis_size("head")
    window_start = first_position - WIN * rows
    starts = (doc_start - window_start).reshape(rows, 1)
    dq, chunks = attention(
        queries.reshape(rows, -1),
        out_grad.reshape(rows, -1),
        pieces,
        starts,
        parts,
    )
    q_grad = dq.reshape(queries.shape)
    k_grad, v_grad = grad_reduce(chunks, window_width, jnp.bfloat16)
    return (q_grad, k_grad, v_grad)


def solution(mesh):
    in_specs = (
        P(("dcn", "blk"), "head", None),
        P(("dcn", "blk"), None),
        P(("dcn", "blk"), None),
        P(("dcn", "blk"), "head", None),
        P(("dcn", "blk")),
    )
    out_specs = (
        P(("dcn", "blk"), "head", None),
        P(("dcn", "blk", "head"), None),
        P(("dcn", "blk", "head"), None),
    )
    return jax.shard_map(body, mesh=mesh, in_specs=in_specs, out_specs=out_specs, check_vma=False)
```
